256 devices in a mesh: grp: 2 (over core), dia: 32 (over y, z), rad: 4 (over x).
Axes of the slice: x: 4, y: 4, z: 8, core: 2. Of those that a mesh axis runs over, the one named last changes fastest.
Arguments:
- thermal_scalar: float32 [16, 2048, 128], P(None, ('grp', 'dia', 'rad')), may hold values from 0.5 to 8.5
- motion_vector_guess: float32 [3, 16, 2048, 128], P(None, 'rad', ('grp', 'dia')), may hold values from -4.5 to 4.5
- mean_stress_guess: float32 [16, 2048, 128], P('rad', ('grp', 'dia')), may hold values from -2 to 4
- flow_resistance_coefficient: float32 [16, 2048, 128], P('rad', ('grp', 'dia')), may hold values from 0.5 to 5
- flipped_junction_flags: int32 [16], replicated, may hold values 0 or 1
Outputs:
- velocity_out: float32 [3, 16, 2048, 128], P(None, 'rad', ('grp', 'dia'))
- pressure_out: float32 [16, 2048, 128], P('rad', ('grp', 'dia'))
- temperature_out: float32 [16, 2048, 128], P(None, ('grp', 'dia', 'rad'))
The draws below stay inside these ranges and needn't reach their ends.
All inputs are finite; a program needn't handle non-finite values.
Results may differ from the reference program's by a relative error of at most 0.0003.
Values sent between devices are 32-bit elements; how exact they have to be, the bound alone decides.
A program may use at most 64 MiB of HBM per device.

```python
import math
from functools import partial
import jax
import jax.numpy as jnp

CROSS_POINT_NUM = 128
DIA_ROWS = 128
SWEEPS = 3
UZAWA = 2
DEPTH_LAYER_NUM = 16
STRIP_LINE_COUNT = 2048
NDIA = 16


def smooth_field(seeded, radial, lateral, across, long_period, weights):
    phases = jax.random.uniform(seeded, (3,), jnp.float32, 0.0, 2.0 * math.pi)
    depth_pos = jnp.arange(radial, dtype=jnp.float32)[:, None, None]
    strip_pos = jnp.arange(lateral, dtype=jnp.float32)[None, :, None]
    cross_pos = jnp.arange(across, dtype=jnp.float32)[None, None, :]
    wave_along = jnp.sin(2.0 * math.pi * strip_pos / long_period + phases[0])
    wave_across = jnp.cos(2.0 * math.pi * cross_pos / across + phases[1])
    wave_depth = jnp.cos(math.pi * depth_pos / radial + phases[2])
    return weights[0] * wave_along + weights[1] * wave_across + weights[2] * wave_depth


def smooth_plus_rough(seeded, center, smooth_amp, rough_amp):
    radial = DEPTH_LAYER_NUM
    lateral = STRIP_LINE_COUNT
    across = CROSS_POINT_NUM
    wave_key = jax.random.fold_in(seeded, 101)
    rough_key = jax.random.fold_in(seeded, 202)
    smooth_part = smooth_field(wave_key, radial, lateral, across, lateral / 4.0, (0.6, 0.25, 0.15))
    rough_part = jnp.clip(jax.random.normal(rough_key, (radial, lateral, across), jnp.float32), -3.0, 3.0)
    return center + smooth_amp * smooth_part + rough_amp * rough_part


def draw_thermal_scalar(key, part):
    seeded = jax.random.fold_in(key, 11)
    return smooth_plus_rough(seeded, 4.5, 1.5, 0.7).astype(jnp.float32)


def draw_motion_vector_guess(key, part):
    centers = (1.5, 1.0, -1.0)
    parts_list = []
    for component in range(3):
        seeded = jax.random.fold_in(key, 31 + component)
        parts_list.append(smooth_plus_rough(seeded, centers[component], 1.0, 0.5))
    return jnp.stack(parts_list, axis=0).astype(jnp.float32)


def draw_mean_stress_guess(key, part):
    seeded = jax.random.fold_in(key, 47)
    return smooth_plus_rough(seeded, 1.0, 1.0, 0.5).astype(jnp.float32)


def touch_ends(drawn, own_key, low, largest):
    dims = drawn.shape
    place = [jax.random.randint(jax.random.fold_in(own_key, axis), (), 0, dims[axis]) for axis in range(len(dims))]
    drawn = drawn.at[tuple(place)].set(low)
    longest = dims.index(max(dims))
    place[longest] = (place[longest] + 1) % dims[longest]
    return drawn.at[tuple(place)].set(largest)


def level_of(rng, dims, split, low, top_value):
    def one(axis_at, shards_of):
        draws = jax.random.uniform(jax.random.fold_in(jax.random.fold_in(rng, 6), axis_at), (shards_of,), jnp.float32, low / len(split), top_value / len(split))
        return jnp.repeat(jnp.exp(draws), dims[axis_at] // shards_of).reshape((-1,) + (1,) * (len(dims) - axis_at - 1))

    factor_of = one(*split[0])
    for cut in split[1:]:
        factor_of = factor_of * one(*cut)
    return factor_of


def setup_inputs(seed: int = 0) -> dict:
    streams_of = jax.random.split(jax.random.key(seed), 6)
    thermal_scalar = draw_thermal_scalar(jax.random.fold_in(streams_of[5], 71), 0)
    motion_vector_guess = draw_motion_vector_guess(jax.random.fold_in(streams_of[5], 71), 0)
    mean_stress_guess = draw_mean_stress_guess(jax.random.fold_in(streams_of[5], 71), 0)
    flow_resistance_coefficient = jnp.clip(jnp.exp(math.log(5.0) - 2.3025851 * jax.random.uniform(streams_of[3], (DEPTH_LAYER_NUM, STRIP_LINE_COUNT, CROSS_POINT_NUM), jnp.float32) ** level_of(streams_of[3], (DEPTH_LAYER_NUM, STRIP_LINE_COUNT, CROSS_POINT_NUM), ((0, 4), (1, 64)), -0.2, 0.2)), 0.5, 5.0)
    flipped_junction_flags = touch_ends((jax.random.randint(streams_of[4], (NDIA,), 0, 2) < 1).astype(jnp.int32), jax.random.fold_in(streams_of[4], 1), 0, 1)
    return dict(thermal_scalar=thermal_scalar, motion_vector_guess=motion_vector_guess, mean_stress_guess=mean_stress_guess, flow_resistance_coefficient=flow_resistance_coefficient, flipped_junction_flags=flipped_junction_flags)


OMEGA = 0.8
TAU = 0.25
RAYLEIGH = 4.0
KAPPA = 1.0
TIME_STEP = 0.1


def laplace(center, neighbours, spacing):
    summed = neighbours[0][0] + neighbours[0][1] + neighbours[1][0] + neighbours[1][1] + neighbours[2][0] + neighbours[2][1]
    return (6.0 * center - summed) / (spacing * spacing)


def gradient(neighbours, spacing):
    return jnp.concatenate([(neighbours[direction][0] - neighbours[direction][1]) / (2.0 * spacing) for direction in range(3)], axis=0)


def divergence(neighbours, spacing):
    summed = (neighbours[0][0][0:1] - neighbours[0][1][0:1]) / (2.0 * spacing)
    summed = summed + (neighbours[1][0][1:2] - neighbours[1][1][1:2]) / (2.0 * spacing)
    summed = summed + (neighbours[2][0][2:3] - neighbours[2][1][2:3]) / (2.0 * spacing)
    return summed


def uzawa_round(flow_field, press_field, forcing, viscous, target, pairs_of, spacing):
    pressure_push = gradient(pairs_of(press_field), spacing)
    for turn_index in range(SWEEPS):
        beside_all = pairs_of(flow_field)
        flow_field = flow_field + OMEGA * (forcing - pressure_push - viscous * laplace(flow_field, beside_all, spacing)) * (spacing * spacing) / (6.0 * viscous)
    beside_all = pairs_of(flow_field)
    press_field = press_field - TAU * viscous * (divergence(beside_all, spacing) + target)
    return flow_field, press_field, beside_all


def whole_pairs(field, seam_table, block):
    zero_rim = jnp.zeros_like(field[:, :1])
    low_r = jnp.concatenate([zero_rim, field[:, :-1]], axis=1)
    high_r = jnp.concatenate([field[:, 1:], zero_rim], axis=1)
    length_a = field.shape[2]
    position = jnp.arange(length_a)
    owner_block = position // block
    blocks = seam_table.shape[0]
    left_raw = jnp.roll(field, 1, axis=2)
    right_raw = jnp.roll(field, -1, axis=2)
    left_seam = (position % block == 0) & (seam_table[owner_block] == 1)
    right_seam = (position % block == block - 1) & (seam_table[(owner_block + 1) % blocks] == 1)
    low_a = jnp.where(left_seam[:, None], left_raw[..., ::-1], left_raw)
    high_a = jnp.where(right_seam[:, None], right_raw[..., ::-1], right_raw)
    zero_side = jnp.zeros_like(field[..., :1])
    low_b = jnp.concatenate([zero_side, field[..., :-1]], axis=3)
    high_b = jnp.concatenate([field[..., 1:], zero_side], axis=3)
    return ((high_r, low_r), (high_a, low_a), (high_b, low_b))


def restrict_coarse(field):
    channels, radial, lateral, across = field.shape
    return field.reshape(channels, radial // 2, 2, lateral // 2, 2, across // 2, 2).mean(axis=(2, 4, 6))


def prolong(field):
    return jnp.repeat(jnp.repeat(jnp.repeat(field, 2, axis=1), 2, axis=2), 2, axis=3)


def reference(thermal_scalar, motion_vector_guess, mean_stress_guess, flow_resistance_coefficient, flipped_junction_flags):
    fine_of = partial(whole_pairs, seam_table=flipped_junction_flags, block=DIA_ROWS)
    coarse_of = partial(whole_pairs, seam_table=flipped_junction_flags, block=DIA_ROWS // 2)
    thermal_state = thermal_scalar[None]
    viscous = flow_resistance_coefficient[None]
    forcing = jnp.concatenate([RAYLEIGH * thermal_state, jnp.zeros_like(motion_vector_guess[1:])], axis=0)
    flow_field, press_field, beside_all = uzawa_round(motion_vector_guess, mean_stress_guess[None], forcing, viscous, 0.0, fine_of, 1.0)
    residual_flow = forcing - gradient(fine_of(press_field), 1.0) - viscous * laplace(flow_field, fine_of(flow_field), 1.0)
    residual_mass = divergence(fine_of(flow_field), 1.0)
    coarse_force = restrict_coarse(residual_flow)
    coarse_target = restrict_coarse(residual_mass)
    coarse_visc = restrict_coarse(viscous)
    correction = jnp.zeros_like(coarse_force)
    pressure_fix = jnp.zeros_like(coarse_target)
    for round_index in range(UZAWA):
        correction, pressure_fix, beside_all = uzawa_round(correction, pressure_fix, coarse_force, coarse_visc, coarse_target, coarse_of, 2.0)
    flow_field = flow_field + prolong(correction)
    press_field = press_field + prolong(pressure_fix)
    flow_field, press_field, beside_all = uzawa_round(flow_field, press_field, forcing, viscous, 0.0, fine_of, 1.0)
    heat_pairs = fine_of(thermal_state)
    carried = jnp.sum(flow_field * gradient(heat_pairs, 1.0), axis=0, keepdims=True)
    heat_next = thermal_state + TIME_STEP * (-KAPPA * laplace(thermal_state, heat_pairs, 1.0) - carried)
    return flow_field, press_field[0], heat_next[0]
```

```python
import functools

import jax
import jax.numpy as jnp
from jax import lax
from jax.experimental import pallas as pl
from jax.experimental.pallas import tpu as pltpu
from jax.sharding import PartitionSpec as P

DIA_ROWS = 128
OMEGA = 0.8
TAU = 0.25
RAYLEIGH = 4.0
KAPPA = 1.0
TIME_STEP = 0.1
MESH = pl.DeviceIdType.MESH

R0 = 8
HU = 5
HE = 4
IN = pl.ds(8, 16)
UP = pl.ds(9, 16)
DN = pl.ds(7, 16)
CIN = pl.ds(8, 8)
CUP = pl.ds(9, 8)
CDN = pl.ds(7, 8)
C0 = 9
A = 1.0 - OMEGA
B = OMEGA / 6.0


def rows(lo, hi, body, unroll=2):
    lax.fori_loop(lo, hi, lambda i, c: (body(i), c)[1], 0, unroll=unroll)


def column(ref, i):
    layers, width, lanes = ref.shape
    return ref.reshape(layers * width, lanes)[pl.ds(i, layers, stride=width)]


def set_column(ref, i, v):
    layers, width, lanes = ref.shape
    ref.reshape(layers * width, lanes)[pl.ds(i, layers, stride=width)] = v


def span(rt, halo):
    lo, hi = max(0, 8 * rt - halo), min(32, 8 * rt + 8 + halo)
    return lo, hi - lo, lo - 8 * rt + R0


def kernel(
    n_dia, n_chain, n_diamonds,
    t_ref, u_ref, p_ref, e_ref, flag_ref,
    uo_ref, po_ref, to_ref,
    rawu, rawp, rawe, rawt,
    U, PB, PF, EB, KB, TB, CB, DB, TMP,
    CS, CR, CU, CC, CE, CG, CP, X, HU_R, HP_R, OUT, TO,
    sgn, csgn, cflip,
    gs, gr, ls, hs, hr, xs, xr, os_, or_, ol,
):
    g = lax.axis_index("grp")
    d = lax.axis_index("dia")
    r = lax.axis_index("rad")
    k = g * n_dia + d
    c = k * 4 + r
    n_k = n_chain // 4

    def dev(ci):
        kk = lax.div(ci, 4)
        return (lax.div(kk, n_dia), lax.rem(kk, n_dia), lax.rem(ci, 4))

    def chain(step):
        return dev(lax.rem(c + step + n_chain, n_chain))

    barrier = pltpu.get_barrier_semaphore()
    for step in (1, -1, 2, -2, 3, -3, 4, -4):
        pl.semaphore_signal(barrier, inc=1, device_id=chain(step), device_id_type=MESH)

    layers = pl.ds(r * 4, 4)
    srcs = ((u_ref, rawu, HU, True), (p_ref, rawp, HU, False), (e_ref, rawe, HE, False))

    def cut(ref, vec, lay, start, size):
        sl = (lay, pl.ds(start, size), slice(None))
        return ref.at[(slice(None),) + sl] if vec else ref.at[sl]

    for rt in range(4):
        @pl.when(r == rt)
        def _():
            for n, (src, dst, halo, vec) in enumerate(srcs):
                lo, size, at = span(rt, halo)
                pltpu.make_async_copy(
                    cut(src, vec, slice(None), lo, size), cut(dst, vec, layers, at, size), ls.at[n]).start()
    pltpu.make_async_copy(t_ref, rawt.at[:, pl.ds(R0, 8)], ls.at[3]).start()

    per = DIA_ROWS // 32
    left = jnp.where((lax.rem(k, per) == 0) & (flag_ref[lax.div(k, per)] == 1), 1, 0)
    right = jnp.where(
        (lax.rem(k + 1, per) == 0) & (flag_ref[lax.rem(lax.div(k + 1, per), n_diamonds)] == 1), 1, 0)

    def flip_of(j, width, block):
        return jnp.where(j < -width * r, left, jnp.where(j >= block - width * r, right, 0))

    for i in range(24):
        sgn[i] = jnp.where(flip_of(i - R0, 8, 32) == 1, -1.0, 1.0)
    for i in range(22):
        csgn[i] = jnp.where(flip_of(i - C0, 4, 16) == 1, -1.0, 1.0)
    for n, J in enumerate((-4, -8, -12, 4, 8, 12)):
        cflip[n] = flip_of(J, 4, 16)
    flip_l, flip_r = flip_of(-1, 8, 32), flip_of(8, 8, 32)

    lane = lax.broadcasted_iota(jnp.int32, (16, 128), 1)
    clane = lax.broadcasted_iota(jnp.int32, (8, 128), 1)
    even = lax.rem(clane, 2) == 0
    back = 127 - lane
    cback = 127 - clane

    def lo1(v):
        return jnp.where(lane == 0, 0.0, pltpu.roll(v, 1, 1))

    def hi1(v):
        return jnp.where(lane == 127, 0.0, pltpu.roll(v, 127, 1))

    def lo2(v):
        return jnp.where(clane < 2, 0.0, pltpu.roll(v, 2, 1))

    def hi2(v):
        return jnp.where(clane >= 126, 0.0, pltpu.roll(v, 126, 1))

    z = jnp.zeros((8, 128), jnp.float32)

    def clear(i):
        for s in range(2):
            for q in range(3):
                U[s, q, i, pl.ds(0, 8)] = z
                U[s, q, i, pl.ds(24, 8)] = z
        for ref in (PB, PF, TB):
            ref[i, pl.ds(0, 8)] = z
            ref[i, pl.ds(24, 8)] = z

    rows(0, 24, clear, 1)

    def cclear(i):
        for s in range(2):
            for q in range(3):
                CU[s, q, i, pl.ds(0, 8)] = z
                CU[s, q, i, pl.ds(16, 8)] = z
        CP[i, pl.ds(0, 8)] = z
        CP[i, pl.ds(16, 8)] = z

    rows(0, 22, cclear, 1)

    pl.semaphore_wait(barrier, 8)

    def remote(src, dst, ssem, rsem, to):
        return pltpu.make_async_remote_copy(
            src_ref=src, dst_ref=dst, send_sem=ssem, recv_sem=rsem, device_id=to, device_id_type=MESH)

    for rt in (0, 1, 2, 3):
        @pl.when(r != rt)
        def _():
            for n, (src, dst, halo, vec) in enumerate(srcs):
                lo, size, at = span(rt, halo)
                remote(cut(src, vec, slice(None), lo, size), cut(dst, vec, layers, at, size),
                       gs.at[n, rt], gr.at[n], (g, d, rt)).start()
    nxt = lax.rem(k + 1, n_k)
    prv = lax.rem(k - 1 + n_k, n_k)
    to_next = (lax.div(nxt, n_dia), lax.rem(nxt, n_dia), 0)
    to_prev = (lax.div(prv, n_dia), lax.rem(prv, n_dia), 3)
    lateral = []
    for n, (src, dst, halo, vec) in enumerate(srcs):
        lateral.append(remote(cut(src, vec, slice(None), 32 - halo, halo), cut(dst, vec, layers, R0 - halo, halo),
                              gs.at[n, 4], gr.at[4 + n], to_next))
        lateral.append(remote(cut(src, vec, slice(None), 0, halo), cut(dst, vec, layers, R0 + 8, halo),
                              gs.at[n, 5], gr.at[4 + n], to_prev))
    lateral.append(remote(t_ref.at[:, pl.ds(8 - HE, HE)], rawt.at[:, pl.ds(R0 - HE, HE)],
                          gs.at[3, 0], gr.at[3], chain(1)))
    lateral.append(remote(t_ref.at[:, pl.ds(0, HE)], rawt.at[:, pl.ds(R0 + 8, HE)],
                          gs.at[3, 1], gr.at[3], chain(-1)))
    for copy in lateral:
        copy.start()

    def landed(ref, sem):
        pltpu.make_async_copy(ref, ref, sem).wait()

    for rt in range(4):
        @pl.when(r == rt)
        def _():
            for n, (src, dst, halo, vec) in enumerate(srcs):
                lo, size, at = span(rt, halo)
                own = cut(dst, vec, slice(0, 4), at, size)
                landed(own, ls.at[n])
                landed(cut(dst, vec, slice(0, 12), at, size), gr.at[n])
                if rt in (0, 3):
                    landed(cut(dst, vec, slice(0, 16), at, halo), gr.at[4 + n])
    landed(rawt.at[:, pl.ds(R0, 8)], ls.at[3])
    landed(rawt.at[:, pl.ds(R0, 2 * HE)], gr.at[3])

    def put(i, turn):
        for q in range(3):
            U[0, q, i, IN] = turn(column(rawu.at[q], i))
        PB[i, IN] = turn(column(rawp, i))
        EB[i] = turn(column(rawe, i))
        TB[i, IN] = turn(column(rawt, i))

    def turned(flag, idx):
        return lambda v: jnp.where(flag == 1, jnp.take_along_axis(v, idx, axis=1), v)

    rows(8, 16, lambda i: put(i, lambda v: v))
    rows(R0 - HU, R0, lambda i: put(i, turned(flip_l, back)), 1)
    rows(R0 + 8, R0 + 8 + HU, lambda i: put(i, turned(flip_r, back)), 1)

    def stencil(ref, s, q, i):
        v = ref[s, q, i, IN]
        total = (ref[s, q, i, UP] + ref[s, q, i, DN]) + (ref[s, q, i + 1, IN] + ref[s, q, i - 1, IN])
        return v, total + (lo1(v) + hi1(v))

    def sweep(s, i):
        for q in range(3):
            v, total = stencil(U, s, q, i)
            U[1 - s, q, i, IN] = A * v + B * total + CB[q, i]

    def slope(ref, i, sign):
        v = ref[i, IN]
        return (ref[i, UP] - ref[i, DN], ref[i + 1, IN] - ref[i - 1, IN], sign * (hi1(v) - lo1(v)))

    def diverge(s, i, sign):
        v = U[s, 2, i, IN]
        return 0.5 * ((U[s, 0, i, UP] - U[s, 0, i, DN]) + (U[s, 1, i + 1, IN] - U[s, 1, i - 1, IN])
                      + sign * (hi1(v) - lo1(v)))

    def push(press, kinv, i):
        gr_, ga_, gb_ = slope(press, i, sgn[i])
        half = -0.5 * kinv
        CB[0, i] = kinv * (RAYLEIGH * TB[i, IN]) + half * gr_
        CB[1, i] = half * ga_
        CB[2, i] = half * gb_

    def first(i):
        kinv = B / EB[i]
        KB[i] = kinv
        push(PB, kinv, i)
        sweep(0, i)

    rows(4, 20, first)
    rows(5, 19, lambda i: sweep(1, i))
    rows(6, 18, lambda i: sweep(0, i))

    def pre_pressure(i):
        div = diverge(1, i, sgn[i])
        DB[i] = div
        PB[i, IN] = PB[i, IN] - TAU * EB[i] * div

    rows(7, 17, pre_pressure)

    def coarse_row(m):
        i = R0 + 2 * m
        acc = [0.0] * 5
        for ii in (i, i + 1):
            gp = slope(PB, ii, 1.0)
            e = EB[ii]
            for q in range(3):
                v, total = stencil(U, 1, q, ii)
                res = -0.5 * gp[q] - e * (6.0 * v - total)
                if q == 0:
                    res = res + RAYLEIGH * TB[ii, IN]
                acc[q] = acc[q] + res
            acc[3] = acc[3] + e
            acc[4] = acc[4] + DB[ii]
        out = []
        for f in range(5):
            TMP[f, m] = acc[f]
        for f in range(5):
            v = TMP[f, m, pl.ds(0, 8, stride=2)] + TMP[f, m, pl.ds(1, 8, stride=2)]
            v = v + jnp.where(even, pltpu.roll(v, 127, 1), pltpu.roll(v, 1, 1))
            out.append(0.125 * v)
        kinv = (4.0 * B) / out[3]
        return [out[0] * kinv, out[1] * kinv, out[2] * kinv, out[3], out[4]]

    def coarse_put(I, vals):
        for q in range(3):
            CU[0, q, I, CIN] = vals[q]
            CC[q, I] = vals[q]
        CE[I] = vals[3]
        CG[I] = vals[4]

    def coarse_pair(h):
        first_row, second_row = coarse_row(2 * h), coarse_row(2 * h + 1)
        for f in range(5):
            CS[f, h] = jnp.where(even, first_row[f], second_row[f])
        coarse_put(C0 + 2 * h, first_row)
        coarse_put(C0 + 2 * h + 1, second_row)

    rows(0, 2, coarse_pair, 1)

    ex = [
        (remote(CS, CR.at[0], xs.at[0], xr.at[0], chain(1)), 1),
        (remote(CS, CR.at[3], xs.at[1], xr.at[3], chain(-1)), 1),
        (remote(CS.at[pl.ds(0, 3)], CR.at[1, pl.ds(0, 3)], xs.at[2], xr.at[1], chain(2)), 1),
        (remote(CS.at[pl.ds(0, 3)], CR.at[4, pl.ds(0, 3)], xs.at[3], xr.at[4], chain(-2)), 1),
        (remote(CS.at[pl.ds(0, 3), pl.ds(1, 1)], CR.at[2, pl.ds(0, 3), pl.ds(1, 1)], xs.at[4], xr.at[2], chain(3)), 1),
        (remote(CS.at[pl.ds(0, 3), pl.ds(0, 1)], CR.at[5, pl.ds(0, 3), pl.ds(0, 1)], xs.at[5], xr.at[5], chain(-3)), 1),
        (remote(CS.at[pl.ds(3, 2), pl.ds(1, 1)], CR.at[1, pl.ds(3, 2), pl.ds(1, 1)], xs.at[6], xr.at[6], chain(2)), 1),
        (remote(CS.at[pl.ds(3, 2), pl.ds(0, 1)], CR.at[4, pl.ds(3, 2), pl.ds(0, 1)], xs.at[7], xr.at[7], chain(-2)), 1),
    ]
    for copy, _ in ex:
        copy.start()
    halo = [
        remote(U.at[1, :, pl.ds(R0 + 4, 2), IN], HU_R.at[0], hs.at[0], hr.at[0], chain(1)),
        remote(U.at[1, :, pl.ds(R0 + 2, 2), IN], HU_R.at[1], hs.at[1], hr.at[1], chain(-1)),
        remote(PB.at[pl.ds(R0 + 4, 3), IN], HP_R.at[0], hs.at[2], hr.at[2], chain(1)),
        remote(PB.at[pl.ds(R0 + 1, 3), IN], HP_R.at[1], hs.at[3], hr.at[3], chain(-1)),
    ]
    for copy in halo:
        copy.start()
    for copy, _ in ex:
        copy.wait_recv()

    def unpack(x):
        return (jnp.where(even, x, pltpu.roll(x, 1, 1)), jnp.where(even, pltpu.roll(x, 127, 1), x))

    def take(n, f, h):
        turn = turned(cflip[n], cback)
        a, b = unpack(CR[n, f, h])
        return turn(a), turn(b)

    for n, base, fulls in ((0, -4, (0, 1)), (3, 4, (0, 1)), (1, -8, (1,)), (4, 8, (0,))):
        for h in (0, 1):
            I = C0 + base + 2 * h
            for q in range(3):
                a, b = take(n, q, h)
                for o, v in ((I, a), (I + 1, b)):
                    CU[0, q, o, CIN] = v
                    CC[q, o] = v
            if h in fulls:
                for f, ref in ((3, CE), (4, CG)):
                    a, b = take(n, f, h)
                    ref[I] = a
                    ref[I + 1] = b
    for q in range(3):
        CU[0, q, 0, CIN] = take(2, q, 1)[1]
        CU[0, q, 21, CIN] = take(5, q, 0)[0]

    def csweep(s, i):
        for q in range(3):
            v = CU[s, q, i, CIN]
            total = (CU[s, q, i, CUP] + CU[s, q, i, CDN]) + (CU[s, q, i + 1, CIN] + CU[s, q, i - 1, CIN])
            CU[1 - s, q, i, CIN] = A * v + B * (total + (lo2(v) + hi2(v))) + CC[q, i]

    def cdiverge(s, i):
        v = CU[s, 2, i, CIN]
        return 0.25 * ((CU[s, 0, i, CUP] - CU[s, 0, i, CDN]) + (CU[s, 1, i + 1, CIN] - CU[s, 1, i - 1, CIN])
                       + csgn[i] * (hi2(v) - lo2(v)))

    rows(1, 21, lambda i: csweep(0, i))
    rows(2, 20, lambda i: csweep(1, i))

    def cpress1(i):
        CP[i, CIN] = -TAU * CE[i] * (cdiverge(0, i) + CG[i])

    rows(3, 19, cpress1)

    def cfirst(i):
        v = CP[i, CIN]
        scale = (-B) / CE[i]
        CC[0, i] = CC[0, i] + scale * (CP[i, CUP] - CP[i, CDN])
        CC[1, i] = CC[1, i] + scale * (CP[i + 1, CIN] - CP[i - 1, CIN])
        CC[2, i] = CC[2, i] + scale * (csgn[i] * (hi2(v) - lo2(v)))
        csweep(0, i)

    rows(4, 18, cfirst)
    rows(5, 17, lambda i: csweep(1, i))
    rows(6, 16, lambda i: csweep(0, i))

    for copy in halo:
        copy.wait_recv()
    for side, flag, urow, prow in ((0, flip_l, 4, 4), (1, flip_r, 18, 17)):
        turn = turned(flag, back)
        for n in range(2):
            for q in range(3):
                U[1, q, urow + n, IN] = turn(HU_R[side, q, n])
        for n in range(3):
            PB[prow + n, IN] = turn(HP_R[side, n])

    def back_up(i):
        m = i - 7
        vals = [CU[1, 0, i, CIN], CU[1, 1, i, CIN], CU[1, 2, i, CIN],
                CP[i, CIN] - TAU * CE[i] * (cdiverge(1, i) + CG[i])]
        for f in range(4):
            X[f, m, pl.ds(0, 8, stride=2)] = vals[f]
            X[f, m, pl.ds(1, 8, stride=2)] = vals[f]
        for f in range(4):
            v = X[f, m]
            for n in range(2):
                row = 4 + 2 * m + n
                if f < 3:
                    U[0, f, row, IN] = U[1, f, row, IN] + v
                else:
                    PF[row, IN] = PB[row, IN] + v

    rows(7, 15, back_up)
    for copy in halo:
        copy.wait_send()

    def last_first(i):
        push(PF, KB[i], i)
        sweep(0, i)

    rows(5, 19, last_first)
    rows(6, 18, lambda i: sweep(1, i))
    rows(7, 17, lambda i: sweep(0, i))

    def finish(a):
        i = R0 + a
        for q in range(3):
            set_column(OUT.at[q], a, U[1, q, i, IN])
        set_column(OUT.at[3], a, PF[i, IN] - TAU * EB[i] * diverge(1, i, 1.0))
        t = TB[i, IN]
        up, dn, nx, pv, hi, lo = TB[i, UP], TB[i, DN], TB[i + 1, IN], TB[i - 1, IN], hi1(t), lo1(t)
        lap = 6.0 * t - (((up + dn) + (nx + pv)) + (hi + lo))
        carried = 0.5 * (U[1, 0, i, IN] * (up - dn) + U[1, 1, i, IN] * (nx - pv) + U[1, 2, i, IN] * (hi - lo))
        set_column(TO, a, t + TIME_STEP * (-KAPPA * lap - carried))

    rows(0, 8, finish)

    mine = pl.ds(pl.multiple_of(r * 8, 8), 8)
    for rt in range(4):
        lay = pl.ds(4 * rt, 4)

        @pl.when(r != rt)
        def _():
            remote(OUT.at[pl.ds(0, 3), lay], uo_ref.at[:, :, mine], os_.at[0, rt], or_.at[0], (g, d, rt)).start()
            remote(OUT.at[3, lay], po_ref.at[:, mine], os_.at[1, rt], or_.at[1], (g, d, rt)).start()

    own_u = pltpu.make_async_copy(OUT.at[pl.ds(0, 3), layers], uo_ref.at[:, :, mine], ol.at[0])
    own_p = pltpu.make_async_copy(OUT.at[3, layers], po_ref.at[:, mine], ol.at[1])
    own_t = pltpu.make_async_copy(TO, to_ref, ol.at[2])
    for copy in (own_u, own_p, own_t):
        copy.start()

    for copy in lateral:
        copy.wait_send()
    for copy, _ in ex:
        copy.wait_send()
    for rt in range(4):
        lay = pl.ds(4 * rt, 4)

        @pl.when(r != rt)
        def _():
            for n, (src, dst, halo_, vec) in enumerate(srcs):
                lo, size, at = span(rt, halo_)
                remote(cut(src, vec, slice(None), lo, size), cut(dst, vec, layers, at, size),
                       gs.at[n, rt], gr.at[n], (g, d, rt)).wait_send()
            remote(OUT.at[pl.ds(0, 3), lay], uo_ref.at[:, :, mine], os_.at[0, rt], or_.at[0], (g, d, rt)).wait_send()
            remote(OUT.at[3, lay], po_ref.at[:, mine], os_.at[1, rt], or_.at[1], (g, d, rt)).wait_send()
    for copy in (own_u, own_p, own_t):
        copy.wait()
    landed(uo_ref.at[:, :, pl.ds(0, 24)], or_.at[0])
    landed(po_ref.at[:, pl.ds(0, 24)], or_.at[1])


def per_device(n_dia, n_chain, t, u, p, e, flags):
    f32 = jnp.float32
    V = pltpu.VMEM
    DMA = pltpu.SemaphoreType.DMA
    any_ = pl.BlockSpec(memory_space=pl.ANY)
    return pl.pallas_call(
        functools.partial(kernel, n_dia, n_chain, flags.shape[0]),
        out_shape=(
            jax.ShapeDtypeStruct(u.shape, f32),
            jax.ShapeDtypeStruct(p.shape, f32),
            jax.ShapeDtypeStruct(t.shape, f32),
        ),
        in_specs=[any_] * 4 + [pl.BlockSpec(memory_space=pltpu.SMEM)],
        out_specs=(any_,) * 3,
        scratch_shapes=[
            V((3, 16, 24, 128), f32), V((16, 24, 128), f32), V((16, 24, 128), f32), V((16, 24, 128), f32),
            V((2, 3, 24, 32, 128), f32), V((24, 32, 128), f32), V((24, 32, 128), f32),
            V((24, 16, 128), f32), V((24, 16, 128), f32), V((24, 32, 128), f32),
            V((3, 24, 16, 128), f32), V((24, 16, 128), f32), V((5, 4, 16, 128), f32),
            V((5, 2, 8, 128), f32), V((6, 5, 2, 8, 128), f32),
            V((2, 3, 22, 24, 128), f32), V((3, 22, 8, 128), f32), V((22, 8, 128), f32), V((22, 8, 128), f32),
            V((22, 24, 128), f32), V((4, 8, 16, 128), f32),
            V((2, 3, 2, 16, 128), f32), V((2, 3, 16, 128), f32),
            V((4, 16, 8, 128), f32), V((16, 8, 128), f32),
            pltpu.SMEM((24,), f32), pltpu.SMEM((22,), f32), pltpu.SMEM((6,), jnp.int32),
            DMA((4, 6)), DMA((7,)), DMA((4,)), DMA((4,)), DMA((4,)), DMA((8,)), DMA((8,)),
            DMA((2, 4)), DMA((2,)), DMA((3,)),
        ],
        compiler_params=pltpu.CompilerParams(collective_id=0, has_side_effects=True),
        name="cycle",
    )(t, u, p, e, flags)


def solution(mesh):
    n_dia = mesh.shape["dia"]
    n_chain = n_dia * mesh.shape["grp"] * mesh.shape["rad"]
    return jax.shard_map(
        functools.partial(per_device, n_dia, n_chain),
        mesh=mesh,
        in_specs=(
            P(None, ("grp", "dia", "rad"), None),
            P(None, "rad", ("grp", "dia"), None),
            P("rad", ("grp", "dia"), None),
            P("rad", ("grp", "dia"), None),
            P(),
        ),
        out_specs=(
            P(None, "rad", ("grp", "dia"), None),
            P("rad", ("grp", "dia"), None),
            P(None, ("grp", "dia", "rad"), None),
        ),
        check_vma=False,
    )
```

```python
import functools

import jax
import jax.numpy as jnp
from jax import lax
from jax.experimental import pallas as pl
from jax.experimental.pallas import tpu as pltpu
from jax.sharding import PartitionSpec as P

DIA_ROWS = 128
OMEGA = 0.8
TAU = 0.25
RAYLEIGH = 4.0
KAPPA = 1.0
TIME_STEP = 0.1
MESH = pl.DeviceIdType.MESH

R0 = 8
HU = 5
HE = 4
IN = pl.ds(8, 16)
UP = pl.ds(9, 16)
DN = pl.ds(7, 16)
CIN = pl.ds(8, 8)
CUP = pl.ds(9, 8)
CDN = pl.ds(7, 8)
C0 = 9
A = 1.0 - OMEGA
B = OMEGA / 6.0


def rows(lo, hi, body, unroll=None):
    unroll = hi - lo if unroll is None else unroll
    lax.fori_loop(lo, hi, lambda i, c: (body(i), c)[1], 0, unroll=unroll)


def column(ref, i):
    layers, width, lanes = ref.shape
    return ref.reshape(layers * width, lanes)[pl.ds(i, layers, stride=width)]


def set_column(ref, i, v):
    layers, width, lanes = ref.shape
    ref.reshape(layers * width, lanes)[pl.ds(i, layers, stride=width)] = v


def span(rt, halo):
    lo, hi = max(0, 8 * rt - halo), min(32, 8 * rt + 8 + halo)
    return lo, hi - lo, lo - 8 * rt + R0


def kernel(
    n_dia, n_chain, n_diamonds,
    t_ref, u_ref, p_ref, e_ref, flag_ref,
    uo_ref, po_ref, to_ref,
    rawu, rawp, rawe, rawt,
    U, PB, PF, EB, KB, TB, CB, DB, TMP,
    CS, CR, CU, CC, CE, CG, CP, X, HU_R, HP_R, OUT,
    sgn, csgn, cflip,
    gs, gr, ls, hs, hr, xs, xr, os_, or_, ol,
):
    g = lax.axis_index("grp")
    d = lax.axis_index("dia")
    r = lax.axis_index("rad")
    k = g * n_dia + d
    c = k * 4 + r
    n_k = n_chain // 4

    def dev(ci):
        kk = lax.div(ci, 4)
        return (lax.div(kk, n_dia), lax.rem(kk, n_dia), lax.rem(ci, 4))

    def chain(step):
        return dev(lax.rem(c + step + n_chain, n_chain))

    barrier = pltpu.get_barrier_semaphore()
    for step in (1, -1, 2, -2, 3, -3, 4, -4):
        pl.semaphore_signal(barrier, inc=1, device_id=chain(step), device_id_type=MESH)

    layers = pl.ds(r * 4, 4)
    srcs = ((p_ref, rawp, HU, False), (e_ref, rawe, HE, False), (u_ref, rawu, HU, True))

    def cut(ref, vec, lay, start, size):
        sl = (lay, pl.ds(start, size), slice(None))
        return ref.at[(slice(None),) + sl] if vec else ref.at[sl]

    for rt in range(4):
        @pl.when(r == rt)
        def _():
            for n, (src, dst, halo, vec) in enumerate(srcs):
                lo, size, at = span(rt, halo)
                pltpu.make_async_copy(
                    cut(src, vec, slice(None), lo, size), cut(dst, vec, layers, at, size), ls.at[n]).start()
    pltpu.make_async_copy(t_ref, rawt.at[:, pl.ds(R0, 8)], ls.at[3]).start()

    per = DIA_ROWS // 32
    left = jnp.where((lax.rem(k, per) == 0) & (flag_ref[lax.div(k, per)] == 1), 1, 0)
    right = jnp.where(
        (lax.rem(k + 1, per) == 0) & (flag_ref[lax.rem(lax.div(k + 1, per), n_diamonds)] == 1), 1, 0)

    def flip_of(j, width, block):
        return jnp.where(j < -width * r, left, jnp.where(j >= block - width * r, right, 0))

    for i in range(24):
        sgn[i] = jnp.where(flip_of(i - R0, 8, 32) == 1, -1.0, 1.0)
    for i in range(22):
        csgn[i] = jnp.where(flip_of(i - C0, 4, 16) == 1, -1.0, 1.0)
    for n, J in enumerate((-4, -8, -12, 4, 8, 12)):
        cflip[n] = flip_of(J, 4, 16)
    flip_l, flip_r = flip_of(-1, 8, 32), flip_of(8, 8, 32)

    lane = lax.broadcasted_iota(jnp.int32, (16, 128), 1)
    clane = lax.broadcasted_iota(jnp.int32, (8, 128), 1)
    even = lax.rem(clane, 2) == 0
    back = 127 - lane
    cback = 127 - clane

    def lo1(v):
        return jnp.where(lane == 0, 0.0, pltpu.roll(v, 1, 1))

    def hi1(v):
        return jnp.where(lane == 127, 0.0, pltpu.roll(v, 127, 1))

    def lo2(v):
        return jnp.where(clane < 2, 0.0, pltpu.roll(v, 2, 1))

    def hi2(v):
        return jnp.where(clane >= 126, 0.0, pltpu.roll(v, 126, 1))

    z = jnp.zeros((8, 128), jnp.float32)

    def clear(i):
        for s in range(2):
            for q in range(3):
                U[s, q, i, pl.ds(0, 8)] = z
                U[s, q, i, pl.ds(24, 8)] = z
        for ref in (PB, PF, TB):
            ref[i, pl.ds(0, 8)] = z
            ref[i, pl.ds(24, 8)] = z

    rows(0, 24, clear, 1)

    def cclear(i):
        for s in range(2):
            for q in range(3):
                CU[s, q, i, pl.ds(0, 8)] = z
                CU[s, q, i, pl.ds(16, 8)] = z
        CP[i, pl.ds(0, 8)] = z
        CP[i, pl.ds(16, 8)] = z

    rows(0, 22, cclear, 1)

    pl.semaphore_wait(barrier, 8)

    def remote(src, dst, ssem, rsem, to):
        return pltpu.make_async_remote_copy(
            src_ref=src, dst_ref=dst, send_sem=ssem, recv_sem=rsem, device_id=to, device_id_type=MESH)

    nxt = lax.rem(k + 1, n_k)
    prv = lax.rem(k - 1 + n_k, n_k)
    to_next = (lax.div(nxt, n_dia), lax.rem(nxt, n_dia), 0)
    to_prev = (lax.div(prv, n_dia), lax.rem(prv, n_dia), 3)
    lateral = []
    for n, (src, dst, halo, vec) in enumerate(srcs):
        here = [
            remote(cut(src, vec, slice(None), 32 - halo, halo), cut(dst, vec, layers, R0 - halo, halo),
                   gs.at[n, 4], gr.at[4 + n], to_next),
            remote(cut(src, vec, slice(None), 0, halo), cut(dst, vec, layers, R0 + 8, halo),
                   gs.at[n, 5], gr.at[4 + n], to_prev)]
        if n == 0:
            here += [
                remote(t_ref.at[:, pl.ds(8 - HE, HE)], rawt.at[:, pl.ds(R0 - HE, HE)], gs.at[3, 0], gr.at[3], chain(1)),
                remote(t_ref.at[:, pl.ds(0, HE)], rawt.at[:, pl.ds(R0 + 8, HE)], gs.at[3, 1], gr.at[3], chain(-1))]
        for copy in here:
            copy.start()
        lateral += here
        for rt in (0, 1, 2, 3):
            @pl.when(r != rt)
            def _():
                lo, size, at = span(rt, halo)
                remote(cut(src, vec, slice(None), lo, size), cut(dst, vec, layers, at, size),
                       gs.at[n, rt], gr.at[n], (g, d, rt)).start()

    def landed(ref, sem):
        pltpu.make_async_copy(ref, ref, sem).wait()

    def gathered(which):
        for rt in range(4):
            @pl.when(r == rt)
            def _():
                for n in which:
                    src, dst, halo, vec = srcs[n]
                    lo, size, at = span(rt, halo)
                    landed(cut(dst, vec, slice(0, 4), at, size), ls.at[n])
                    landed(cut(dst, vec, slice(0, 12), at, size), gr.at[n])
                    if rt in (0, 3):
                        landed(cut(dst, vec, slice(0, 16), at, halo), gr.at[4 + n])

    gathered((0, 1))
    landed(rawt.at[:, pl.ds(R0, 8)], ls.at[3])
    landed(rawt.at[:, pl.ds(R0, 2 * HE)], gr.at[3])

    def put_scalars(i, turn):
        PB[i, IN] = turn(column(rawp, i))
        EB[i] = turn(column(rawe, i))
        TB[i, IN] = turn(column(rawt, i))

    def put_vector(i, turn):
        for q in range(3):
            U[0, q, i, IN] = turn(column(rawu.at[q], i))

    def turned(flag, idx):
        return lambda v: jnp.where(flag == 1, jnp.take_along_axis(v, idx, axis=1), v)

    def put_all(put):
        rows(8, 16, lambda i: put(i, lambda v: v))
        rows(R0 - HU, R0, lambda i: put(i, turned(flip_l, back)))
        rows(R0 + 8, R0 + 8 + HU, lambda i: put(i, turned(flip_r, back)))

    put_all(put_scalars)

    def stencil(ref, s, q, i):
        v = ref[s, q, i, IN]
        total = (ref[s, q, i, UP] + ref[s, q, i, DN]) + (ref[s, q, i + 1, IN] + ref[s, q, i - 1, IN])
        return v, total + (lo1(v) + hi1(v))

    def sweep(s, i):
        for q in range(3):
            v, total = stencil(U, s, q, i)
            U[1 - s, q, i, IN] = A * v + B * total + CB[q, i]

    def slope(ref, i, sign):
        v = ref[i, IN]
        return (ref[i, UP] - ref[i, DN], ref[i + 1, IN] - ref[i - 1, IN], sign * (hi1(v) - lo1(v)))

    def diverge(s, i, sign):
        v = U[s, 2, i, IN]
        return 0.5 * ((U[s, 0, i, UP] - U[s, 0, i, DN]) + (U[s, 1, i + 1, IN] - U[s, 1, i - 1, IN])
                      + sign * (hi1(v) - lo1(v)))

    def push(press, kinv, i):
        gr_, ga_, gb_ = slope(press, i, sgn[i])
        half = -0.5 * kinv
        CB[0, i] = kinv * (RAYLEIGH * TB[i, IN]) + half * gr_
        CB[1, i] = half * ga_
        CB[2, i] = half * gb_

    def first_push(i):
        kinv = B / EB[i]
        KB[i] = kinv
        push(PB, kinv, i)

    rows(4, 20, first_push)
    gathered((2,))
    put_all(put_vector)
    rows(4, 20, lambda i: sweep(0, i))
    rows(5, 19, lambda i: sweep(1, i))
    rows(6, 18, lambda i: sweep(0, i))

    def pre_pressure(i):
        div = diverge(1, i, sgn[i])
        DB[i] = div
        PB[i, IN] = PB[i, IN] - TAU * EB[i] * div

    rows(7, 17, pre_pressure)

    def coarse_row(m):
        i = R0 + 2 * m
        acc = [0.0] * 5
        for ii in (i, i + 1):
            gp = slope(PB, ii, 1.0)
            e = EB[ii]
            for q in range(3):
                v, total = stencil(U, 1, q, ii)
                res = -0.5 * gp[q] - e * (6.0 * v - total)
                if q == 0:
                    res = res + RAYLEIGH * TB[ii, IN]
                acc[q] = acc[q] + res
            acc[3] = acc[3] + e
            acc[4] = acc[4] + DB[ii]
        out = []
        for f in range(5):
            TMP[f, m] = acc[f]
        for f in range(5):
            v = TMP[f, m, pl.ds(0, 8, stride=2)] + TMP[f, m, pl.ds(1, 8, stride=2)]
            v = v + jnp.where(even, pltpu.roll(v, 127, 1), pltpu.roll(v, 1, 1))
            out.append(0.125 * v)
        kinv = (4.0 * B) / out[3]
        return [out[0] * kinv, out[1] * kinv, out[2] * kinv, out[3], out[4]]

    def coarse_put(I, vals):
        for q in range(3):
            CU[0, q, I, CIN] = vals[q]
            CC[q, I] = vals[q]
        CE[I] = vals[3]
        CG[I] = vals[4]

    def coarse_pair(h):
        first_row, second_row = coarse_row(2 * h), coarse_row(2 * h + 1)
        for f in range(5):
            CS[f, h] = jnp.where(even, first_row[f], second_row[f])
        coarse_put(C0 + 2 * h, first_row)
        coarse_put(C0 + 2 * h + 1, second_row)

    rows(0, 2, coarse_pair)

    ex = [
        (remote(CS, CR.at[0], xs.at[0], xr.at[0], chain(1)), 1),
        (remote(CS, CR.at[3], xs.at[1], xr.at[3], chain(-1)), 1),
        (remote(CS.at[pl.ds(0, 3)], CR.at[1, pl.ds(0, 3)], xs.at[2], xr.at[1], chain(2)), 1),
        (remote(CS.at[pl.ds(0, 3)], CR.at[4, pl.ds(0, 3)], xs.at[3], xr.at[4], chain(-2)), 1),
        (remote(CS.at[pl.ds(0, 3), pl.ds(1, 1)], CR.at[2, pl.ds(0, 3), pl.ds(1, 1)], xs.at[4], xr.at[2], chain(3)), 1),
        (remote(CS.at[pl.ds(0, 3), pl.ds(0, 1)], CR.at[5, pl.ds(0, 3), pl.ds(0, 1)], xs.at[5], xr.at[5], chain(-3)), 1),
        (remote(CS.at[pl.ds(3, 2), pl.ds(1, 1)], CR.at[1, pl.ds(3, 2), pl.ds(1, 1)], xs.at[6], xr.at[6], chain(2)), 1),
        (remote(CS.at[pl.ds(3, 2), pl.ds(0, 1)], CR.at[4, pl.ds(3, 2), pl.ds(0, 1)], xs.at[7], xr.at[7], chain(-2)), 1),
    ]
    for copy, _ in ex:
        copy.start()
    halo = [
        remote(U.at[1, :, pl.ds(R0 + 4, 2), IN], HU_R.at[0], hs.at[0], hr.at[0], chain(1)),
        remote(U.at[1, :, pl.ds(R0 + 2, 2), IN], HU_R.at[1], hs.at[1], hr.at[1], chain(-1)),
        remote(PB.at[pl.ds(R0 + 4, 3), IN], HP_R.at[0], hs.at[2], hr.at[2], chain(1)),
        remote(PB.at[pl.ds(R0 + 1, 3), IN], HP_R.at[1], hs.at[3], hr.at[3], chain(-1)),
    ]
    for copy in halo:
        copy.start()
    for copy, _ in ex:
        copy.wait_recv()

    def unpack(x):
        return (jnp.where(even, x, pltpu.roll(x, 1, 1)), jnp.where(even, pltpu.roll(x, 127, 1), x))

    def take(n, f, h):
        turn = turned(cflip[n], cback)
        a, b = unpack(CR[n, f, h])
        return turn(a), turn(b)

    for n, base, fulls in ((0, -4, (0, 1)), (3, 4, (0, 1)), (1, -8, (1,)), (4, 8, (0,))):
        for h in (0, 1):
            I = C0 + base + 2 * h
            for q in range(3):
                a, b = take(n, q, h)
                for o, v in ((I, a), (I + 1, b)):
                    CU[0, q, o, CIN] = v
                    CC[q, o] = v
            if h in fulls:
                for f, ref in ((3, CE), (4, CG)):
                    a, b = take(n, f, h)
                    ref[I] = a
                    ref[I + 1] = b
    for q in range(3):
        CU[0, q, 0, CIN] = take(2, q, 1)[1]
        CU[0, q, 21, CIN] = take(5, q, 0)[0]

    def csweep(s, i):
        for q in range(3):
            v = CU[s, q, i, CIN]
            total = (CU[s, q, i, CUP] + CU[s, q, i, CDN]) + (CU[s, q, i + 1, CIN] + CU[s, q, i - 1, CIN])
            CU[1 - s, q, i, CIN] = A * v + B * (total + (lo2(v) + hi2(v))) + CC[q, i]

    def cdiverge(s, i):
        v = CU[s, 2, i, CIN]
        return 0.25 * ((CU[s, 0, i, CUP] - CU[s, 0, i, CDN]) + (CU[s, 1, i + 1, CIN] - CU[s, 1, i - 1, CIN])
                       + csgn[i] * (hi2(v) - lo2(v)))

    rows(1, 21, lambda i: csweep(0, i))
    rows(2, 20, lambda i: csweep(1, i))

    def cpress1(i):
        CP[i, CIN] = -TAU * CE[i] * (cdiverge(0, i) + CG[i])

    rows(3, 19, cpress1)

    def cfirst(i):
        v = CP[i, CIN]
        scale = (-B) / CE[i]
        CC[0, i] = CC[0, i] + scale * (CP[i, CUP] - CP[i, CDN])
        CC[1, i] = CC[1, i] + scale * (CP[i + 1, CIN] - CP[i - 1, CIN])
        CC[2, i] = CC[2, i] + scale * (csgn[i] * (hi2(v) - lo2(v)))
        csweep(0, i)

    rows(4, 18, cfirst)
    rows(5, 17, lambda i: csweep(1, i))
    rows(6, 16, lambda i: csweep(0, i))

    for copy in halo:
        copy.wait_recv()
    for side, flag, urow, prow in ((0, flip_l, 4, 4), (1, flip_r, 18, 17)):
        turn = turned(flag, back)
        for n in range(2):
            for q in range(3):
                U[1, q, urow + n, IN] = turn(HU_R[side, q, n])
        for n in range(3):
            PB[prow + n, IN] = turn(HP_R[side, n])

    def back_up(i):
        m = i - 7
        vals = [CU[1, 0, i, CIN], CU[1, 1, i, CIN], CU[1, 2, i, CIN],
                CP[i, CIN] - TAU * CE[i] * (cdiverge(1, i) + CG[i])]
        for f in range(4):
            X[f, m, pl.ds(0, 8, stride=2)] = vals[f]
            X[f, m, pl.ds(1, 8, stride=2)] = vals[f]
        for f in range(4):
            v = X[f, m]
            for n in range(2):
                row = 4 + 2 * m + n
                if f < 3:
                    U[0, f, row, IN] = U[1, f, row, IN] + v
                else:
                    PF[row, IN] = PB[row, IN] + v

    rows(7, 15, back_up)
    for copy in halo:
        copy.wait_send()

    def last_first(i):
        push(PF, KB[i], i)
        sweep(0, i)

    rows(5, 19, last_first)
    rows(6, 18, lambda i: sweep(1, i))
    rows(7, 17, lambda i: sweep(0, i))

    def finish_u(a):
        for q in range(3):
            set_column(OUT.at[q], a, U[1, q, R0 + a, IN])

    def finish_p(a):
        i = R0 + a
        set_column(OUT.at[3], a, PF[i, IN] - TAU * EB[i] * diverge(1, i, 1.0))

    def finish_t(a):
        i = R0 + a
        t = TB[i, IN]
        up, dn, nx, pv, hi, lo = TB[i, UP], TB[i, DN], TB[i + 1, IN], TB[i - 1, IN], hi1(t), lo1(t)
        lap = 6.0 * t - (((up + dn) + (nx + pv)) + (hi + lo))
        carried = 0.5 * (U[1, 0, i, IN] * (up - dn) + U[1, 1, i, IN] * (nx - pv) + U[1, 2, i, IN] * (hi - lo))
        set_column(to_ref, a, t + TIME_STEP * (-KAPPA * lap - carried))

    mine = pl.ds(pl.multiple_of(r * 8, 8), 8)
    own_u = pltpu.make_async_copy(OUT.at[pl.ds(0, 3), layers], uo_ref.at[:, :, mine], ol.at[0])
    own_p = pltpu.make_async_copy(OUT.at[3, layers], po_ref.at[:, mine], ol.at[1])

    def home_u(rt):
        return remote(OUT.at[pl.ds(0, 3), pl.ds(4 * rt, 4)], uo_ref.at[:, :, mine], os_.at[0, rt], or_.at[0], (g, d, rt))

    def home_p(rt):
        return remote(OUT.at[3, pl.ds(4 * rt, 4)], po_ref.at[:, mine], os_.at[1, rt], or_.at[1], (g, d, rt))

    for finish, home, own in ((finish_u, home_u, own_u), (finish_p, home_p, own_p)):
        rows(0, 8, finish)
        for rt in range(4):
            @pl.when(r != rt)
            def _():
                home(rt).start()
        own.start()
    rows(0, 8, finish_t)

    for copy in lateral:
        copy.wait_send()
    for copy, _ in ex:
        copy.wait_send()
    for rt in range(4):
        @pl.when(r != rt)
        def _():
            for n, (src, dst, halo_, vec) in enumerate(srcs):
                lo, size, at = span(rt, halo_)
                remote(cut(src, vec, slice(None), lo, size), cut(dst, vec, layers, at, size),
                       gs.at[n, rt], gr.at[n], (g, d, rt)).wait_send()
            home_u(rt).wait_send()
            home_p(rt).wait_send()
    for copy in (own_u, own_p):
        copy.wait()
    landed(uo_ref.at[:, :, pl.ds(0, 24)], or_.at[0])
    landed(po_ref.at[:, pl.ds(0, 24)], or_.at[1])


def write_out(*refs):
    sem = refs[6]
    copies = [pltpu.make_async_copy(refs[n], refs[3 + n], sem.at[n]) for n in range(3)]
    for copy in copies:
        copy.start()
    for copy in copies:
        copy.wait()


def per_device(n_dia, n_chain, t, u, p, e, flags):
    f32 = jnp.float32
    V = pltpu.VMEM
    DMA = pltpu.SemaphoreType.DMA
    any_ = pl.BlockSpec(memory_space=pl.ANY)
    vmem = pl.BlockSpec(memory_space=pltpu.VMEM)
    done = pl.pallas_call(
        functools.partial(kernel, n_dia, n_chain, flags.shape[0]),
        out_shape=(
            V(u.shape, f32),
            V(p.shape, f32),
            V(t.shape, f32),
        ),
        in_specs=[any_] * 4 + [pl.BlockSpec(memory_space=pltpu.SMEM)],
        out_specs=(vmem,) * 3,
        scratch_shapes=[
            V((3, 16, 24, 128), f32), V((16, 24, 128), f32), V((16, 24, 128), f32), V((16, 24, 128), f32),
            V((2, 3, 24, 32, 128), f32), V((24, 32, 128), f32), V((24, 32, 128), f32),
            V((24, 16, 128), f32), V((24, 16, 128), f32), V((24, 32, 128), f32),
            V((3, 24, 16, 128), f32), V((24, 16, 128), f32), V((5, 4, 16, 128), f32),
            V((5, 2, 8, 128), f32), V((6, 5, 2, 8, 128), f32),
            V((2, 3, 22, 24, 128), f32), V((3, 22, 8, 128), f32), V((22, 8, 128), f32), V((22, 8, 128), f32),
            V((22, 24, 128), f32), V((4, 8, 16, 128), f32),
            V((2, 3, 2, 16, 128), f32), V((2, 3, 16, 128), f32),
            V((4, 16, 8, 128), f32),
            pltpu.SMEM((24,), f32), pltpu.SMEM((22,), f32), pltpu.SMEM((6,), jnp.int32),
            DMA((4, 6)), DMA((7,)), DMA((4,)), DMA((4,)), DMA((4,)), DMA((8,)), DMA((8,)),
            DMA((2, 4)), DMA((2,)), DMA((2,)),
        ],
        compiler_params=pltpu.CompilerParams(collective_id=0, has_side_effects=True),
        name="cycle",
    )(t, u, p, e, flags)
    return pl.pallas_call(
        write_out,
        out_shape=[jax.ShapeDtypeStruct(x.shape, f32) for x in done],
        in_specs=[vmem] * 3,
        out_specs=[any_] * 3,
        scratch_shapes=[DMA((3,))],
        name="write_out",
    )(*[pltpu.with_memory_space_constraint(x, pltpu.VMEM) for x in done])


def solution(mesh):
    n_dia = mesh.shape["dia"]
    n_chain = n_dia * mesh.shape["grp"] * mesh.shape["rad"]
    return jax.shard_map(
        functools.partial(per_device, n_dia, n_chain),
        mesh=mesh,
        in_specs=(
            P(None, ("grp", "dia", "rad"), None),
            P(None, "rad", ("grp", "dia"), None),
            P("rad", ("grp", "dia"), None),
            P("rad", ("grp", "dia"), None),
            P(),
        ),
        out_specs=(
            P(None, "rad", ("grp", "dia"), None),
            P("rad", ("grp", "dia"), None),
            P(None, ("grp", "dia", "rad"), None),
        ),
        check_vma=False,
    )
```

```python
import functools

import jax
import jax.numpy as jnp
from jax import lax
from jax.experimental import pallas as pl
from jax.experimental.pallas import tpu as pltpu
from jax.sharding import PartitionSpec as P

DIA_ROWS = 128
OMEGA = 0.8
TAU = 0.25
RAYLEIGH = 4.0
KAPPA = 1.0
TIME_STEP = 0.1
MESH = pl.DeviceIdType.MESH

R0 = 8
HU = 5
HE = 4
IN = pl.ds(8, 16)
UP = pl.ds(9, 16)
DN = pl.ds(7, 16)
CIN = pl.ds(8, 8)
CUP = pl.ds(9, 8)
CDN = pl.ds(7, 8)
C0 = 9
A = 1.0 - OMEGA
B = OMEGA / 6.0


def rows(lo, hi, body, unroll=None):
    unroll = hi - lo if unroll is None else unroll
    lax.fori_loop(lo, hi, lambda i, c: (body(i), c)[1], 0, unroll=unroll)


def column(ref, i):
    layers, width, lanes = ref.shape
    return ref.reshape(layers * width, lanes)[pl.ds(i, layers, stride=width)]


def set_column(ref, i, v):
    layers, width, lanes = ref.shape
    ref.reshape(layers * width, lanes)[pl.ds(i, layers, stride=width)] = v


def span(rt, halo):
    lo, hi = max(0, 8 * rt - halo), min(32, 8 * rt + 8 + halo)
    return lo, hi - lo, lo - 8 * rt + R0


def kernel(
    n_dia, n_chain, n_diamonds,
    t_ref, u_ref, p_ref, e_ref, flag_hbm,
    uo_ref, po_ref, to_ref,
    rawu, rawp, rawe, rawt,
    U, PB, PF, EB, KB, TB, CB, DB, TMP,
    CS, CR, CU, CC, CE, CG, CP, X, HU_R, HP_R, OUT,
    flag_ref, sgn, csgn, cflip,
    gs, gr, ls, hs, hr, xs, xr, os_, or_, ol, fs,
):
    g = lax.axis_index("grp")
    d = lax.axis_index("dia")
    r = lax.axis_index("rad")
    k = g * n_dia + d
    c = k * 4 + r
    n_k = n_chain // 4

    def dev(ci):
        kk = lax.div(ci, 4)
        return (lax.div(kk, n_dia), lax.rem(kk, n_dia), lax.rem(ci, 4))

    def chain(step):
        return dev(lax.rem(c + step + n_chain, n_chain))

    barrier = pltpu.get_barrier_semaphore()
    for step in (1, -1, 2, -2, 3, -3, 4, -4):
        pl.semaphore_signal(barrier, inc=1, device_id=chain(step), device_id_type=MESH)

    pl.semaphore_wait(barrier, 8)

    layers = pl.ds(r * 4, 4)
    srcs = ((p_ref, rawp, HU), (e_ref, rawe, HE)) + tuple((u_ref.at[q], rawu.at[q], HU) for q in range(3))

    def cut(ref, lay, start, size):
        return ref.at[lay, pl.ds(start, size)]

    def remote(src, dst, ssem, rsem, to):
        return pltpu.make_async_remote_copy(
            src_ref=src, dst_ref=dst, send_sem=ssem, recv_sem=rsem, device_id=to, device_id_type=MESH)

    nxt = lax.rem(k + 1, n_k)
    prv = lax.rem(k - 1 + n_k, n_k)
    to_next = (lax.div(nxt, n_dia), lax.rem(nxt, n_dia), 0)
    to_prev = (lax.div(prv, n_dia), lax.rem(prv, n_dia), 3)

    def lateral(n):
        src, dst, halo = srcs[n]
        return [
            remote(cut(src, slice(None), 32 - halo, halo), cut(dst, layers, R0 - halo, halo),
                   gs.at[n, 4], gr.at[5 + n], to_next),
            remote(cut(src, slice(None), 0, halo), cut(dst, layers, R0 + 8, halo),
                   gs.at[n, 5], gr.at[5 + n], to_prev)]

    def across(n, rt):
        src, dst, halo = srcs[n]
        lo, size, at = span(rt, halo)
        return remote(cut(src, slice(None), lo, size), cut(dst, layers, at, size), gs.at[n, rt], gr.at[n], (g, d, rt))

    heat = [
        remote(t_ref.at[:, pl.ds(8 - HE, HE)], rawt.at[:, pl.ds(R0 - HE, HE)], gs.at[5, 0], gr.at[10], chain(1)),
        remote(t_ref.at[:, pl.ds(0, HE)], rawt.at[:, pl.ds(R0 + 8, HE)], gs.at[5, 1], gr.at[10], chain(-1))]
    for rs in range(4):
        @pl.when(r == rs)
        def _():
            for n in range(5):
                for copy in lateral(n):
                    copy.start()
                for step in (2, 1, 3):
                    across(n, (rs + step) % 4).start()
                if n == 1:
                    for copy in heat:
                        copy.start()

    read_flags = pltpu.make_async_copy(flag_hbm, flag_ref, fs)
    read_flags.start()
    for rt in range(4):
        @pl.when(r == rt)
        def _():
            for n, (src, dst, halo) in enumerate(srcs):
                lo, size, at = span(rt, halo)
                pltpu.make_async_copy(cut(src, slice(None), lo, size), cut(dst, layers, at, size), ls.at[n]).start()
    pltpu.make_async_copy(t_ref, rawt.at[:, pl.ds(R0, 8)], ls.at[5]).start()

    z = jnp.zeros((8, 128), jnp.float32)

    def clear(i):
        for s in range(2):
            for q in range(3):
                U[s, q, i, pl.ds(0, 8)] = z
                U[s, q, i, pl.ds(24, 8)] = z
        for ref in (PB, PF, TB):
            ref[i, pl.ds(0, 8)] = z
            ref[i, pl.ds(24, 8)] = z

    rows(0, 24, clear, 1)

    def cclear(i):
        for s in range(2):
            for q in range(3):
                CU[s, q, i, pl.ds(0, 8)] = z
                CU[s, q, i, pl.ds(16, 8)] = z
        CP[i, pl.ds(0, 8)] = z
        CP[i, pl.ds(16, 8)] = z

    rows(0, 22, cclear, 1)

    read_flags.wait()
    per = DIA_ROWS // 32
    left = jnp.where((lax.rem(k, per) == 0) & (flag_ref[lax.div(k, per)] == 1), 1, 0)
    right = jnp.where(
        (lax.rem(k + 1, per) == 0) & (flag_ref[lax.rem(lax.div(k + 1, per), n_diamonds)] == 1), 1, 0)

    def flip_of(j, width, block):
        return jnp.where(j < -width * r, left, jnp.where(j >= block - width * r, right, 0))

    for i in range(24):
        sgn[i] = jnp.where(flip_of(i - R0, 8, 32) == 1, -1.0, 1.0)
    for i in range(22):
        csgn[i] = jnp.where(flip_of(i - C0, 4, 16) == 1, -1.0, 1.0)
    for n, J in enumerate((-4, -8, -12, 4, 8, 12)):
        cflip[n] = flip_of(J, 4, 16)
    flip_l, flip_r = flip_of(-1, 8, 32), flip_of(8, 8, 32)

    lane = lax.broadcasted_iota(jnp.int32, (16, 128), 1)
    clane = lax.broadcasted_iota(jnp.int32, (8, 128), 1)
    even = lax.rem(clane, 2) == 0
    back = 127 - lane
    cback = 127 - clane

    def lo1(v):
        return jnp.where(lane == 0, 0.0, pltpu.roll(v, 1, 1))

    def hi1(v):
        return jnp.where(lane == 127, 0.0, pltpu.roll(v, 127, 1))

    def lo2(v):
        return jnp.where(clane < 2, 0.0, pltpu.roll(v, 2, 1))

    def hi2(v):
        return jnp.where(clane >= 126, 0.0, pltpu.roll(v, 126, 1))

    def landed(ref, sem):
        pltpu.make_async_copy(ref, ref, sem).wait()

    def gathered(which):
        for rt in range(4):
            @pl.when(r == rt)
            def _():
                for n in which:
                    src, dst, halo = srcs[n]
                    lo, size, at = span(rt, halo)
                    landed(cut(dst, slice(0, 4), at, size), ls.at[n])
                    landed(cut(dst, slice(0, 12), at, size), gr.at[n])
                    if rt in (0, 3):
                        landed(cut(dst, slice(0, 16), at, halo), gr.at[5 + n])

    gathered((0, 1))
    landed(rawt.at[:, pl.ds(R0, 8)], ls.at[5])
    landed(rawt.at[:, pl.ds(R0, 2 * HE)], gr.at[10])

    def put_scalars(i, turn):
        PB[i, IN] = turn(column(rawp, i))
        EB[i] = turn(column(rawe, i))
        TB[i, IN] = turn(column(rawt, i))

    def put_vector(q, i, turn):
        U[0, q, i, IN] = turn(column(rawu.at[q], i))

    def turned(flag, idx):
        return lambda v: jnp.where(flag == 1, jnp.take_along_axis(v, idx, axis=1), v)

    def put_all(put):
        rows(8, 16, lambda i: put(i, lambda v: v))
        rows(R0 - HU, R0, lambda i: put(i, turned(flip_l, back)))
        rows(R0 + 8, R0 + 8 + HU, lambda i: put(i, turned(flip_r, back)))

    put_all(put_scalars)

    def stencil(ref, s, q, i):
        v = ref[s, q, i, IN]
        total = (ref[s, q, i, UP] + ref[s, q, i, DN]) + (ref[s, q, i + 1, IN] + ref[s, q, i - 1, IN])
        return v, total + (lo1(v) + hi1(v))

    def sweep(s, q, i):
        v, total = stencil(U, s, q, i)
        U[1 - s, q, i, IN] = A * v + B * total + CB[q, i]

    def slope(ref, i, sign):
        v = ref[i, IN]
        return (ref[i, UP] - ref[i, DN], ref[i + 1, IN] - ref[i - 1, IN], sign * (hi1(v) - lo1(v)))

    def diverge(s, i, sign):
        v = U[s, 2, i, IN]
        return 0.5 * ((U[s, 0, i, UP] - U[s, 0, i, DN]) + (U[s, 1, i + 1, IN] - U[s, 1, i - 1, IN])
                      + sign * (hi1(v) - lo1(v)))

    def push(press, kinv, i):
        gr_, ga_, gb_ = slope(press, i, sgn[i])
        half = -0.5 * kinv
        CB[0, i] = kinv * (RAYLEIGH * TB[i, IN]) + half * gr_
        CB[1, i] = half * ga_
        CB[2, i] = half * gb_

    def first_push(i):
        kinv = B / EB[i]
        KB[i] = kinv
        push(PB, kinv, i)

    rows(4, 20, first_push)
    for q in range(3):
        gathered((2 + q,))
        put_all(functools.partial(put_vector, q))
        rows(4, 20, lambda i: sweep(0, q, i))
        rows(5, 19, lambda i: sweep(1, q, i))
        rows(6, 18, lambda i: sweep(0, q, i))

    halo = []
    for q in range(3):
        halo.append((remote(U.at[1, q, pl.ds(R0 + 4, 2), IN], HU_R.at[0, q], hs.at[2 * q], hr.at[2 * q], chain(1)),
                     remote(U.at[1, q, pl.ds(R0 + 2, 2), IN], HU_R.at[1, q], hs.at[2 * q + 1], hr.at[2 * q + 1], chain(-1))))
    halo.append((remote(PB.at[pl.ds(R0 + 4, 3), IN], HP_R.at[0], hs.at[6], hr.at[6], chain(1)),
                 remote(PB.at[pl.ds(R0 + 1, 3), IN], HP_R.at[1], hs.at[7], hr.at[7], chain(-1))))
    for pair in halo[:3]:
        for copy in pair:
            copy.start()

    def pre_pressure(i):
        div = diverge(1, i, sgn[i])
        DB[i] = div
        PB[i, IN] = PB[i, IN] - TAU * EB[i] * div

    rows(7, 17, pre_pressure)
    for copy in halo[3]:
        copy.start()

    def restrict(f, m, acc):
        TMP[f, m] = acc
        v = TMP[f, m, pl.ds(0, 8, stride=2)] + TMP[f, m, pl.ds(1, 8, stride=2)]
        return 0.125 * (v + jnp.where(even, pltpu.roll(v, 127, 1), pltpu.roll(v, 1, 1)))

    def pack(f, vals):
        for h in range(2):
            CS[f, h] = jnp.where(even, vals[2 * h], vals[2 * h + 1])

    def residual(q, ii):
        v, total = stencil(U, 1, q, ii)
        w = PB[ii, IN]
        if q == 0:
            gp = PB[ii, UP] - PB[ii, DN]
        elif q == 1:
            gp = PB[ii + 1, IN] - PB[ii - 1, IN]
        else:
            gp = hi1(w) - lo1(w)
        res = -0.5 * gp - EB[ii] * (6.0 * v - total)
        return res + RAYLEIGH * TB[ii, IN] if q == 0 else res

    def send_vector(q):
        one = pl.ds(q, 1)
        out = [
            remote(CS.at[one], CR.at[1, one], xs.at[q, 1], xr.at[q, 1], chain(2)),
            remote(CS.at[one], CR.at[4, one], xs.at[q, 4], xr.at[q, 4], chain(-2)),
            remote(CS.at[one, pl.ds(1, 1)], CR.at[2, one, pl.ds(1, 1)], xs.at[q, 2], xr.at[q, 2], chain(3)),
            remote(CS.at[one, pl.ds(0, 1)], CR.at[5, one, pl.ds(0, 1)], xs.at[q, 5], xr.at[q, 5], chain(-3)),
            remote(CS.at[one], CR.at[0, one], xs.at[q, 0], xr.at[q, 0], chain(1)),
            remote(CS.at[one], CR.at[3, one], xs.at[q, 3], xr.at[q, 3], chain(-1)),
        ]
        for copy in out:
            copy.start()
        return out

    ce = [restrict(3, m, EB[R0 + 2 * m] + EB[R0 + 2 * m + 1]) for m in range(4)]
    cg = [restrict(4, m, DB[R0 + 2 * m] + DB[R0 + 2 * m + 1]) for m in range(4)]
    cinv = [(4.0 * B) / e for e in ce]
    ex = []
    for q in range(3):
        vals = [cinv[m] * restrict(q, m, residual(q, R0 + 2 * m) + residual(q, R0 + 2 * m + 1)) for m in range(4)]
        pack(q, vals)
        ex.append(send_vector(q))
        for m in range(4):
            CU[0, q, C0 + m, CIN] = vals[m]
            CC[q, C0 + m] = vals[m]
    pack(3, ce)
    pack(4, cg)
    both = pl.ds(3, 2)
    ex.append([
        remote(CS.at[both, pl.ds(1, 1)], CR.at[1, both, pl.ds(1, 1)], xs.at[3, 1], xr.at[3, 1], chain(2)),
        remote(CS.at[both, pl.ds(0, 1)], CR.at[4, both, pl.ds(0, 1)], xs.at[3, 4], xr.at[3, 4], chain(-2)),
        remote(CS.at[both], CR.at[0, both], xs.at[3, 0], xr.at[3, 0], chain(1)),
        remote(CS.at[both], CR.at[3, both], xs.at[3, 3], xr.at[3, 3], chain(-1)),
    ])
    for copy in ex[3]:
        copy.start()
    for m in range(4):
        CE[C0 + m] = ce[m]
        CG[C0 + m] = cg[m]

    def unpack(x):
        return (jnp.where(even, x, pltpu.roll(x, 1, 1)), jnp.where(even, pltpu.roll(x, 127, 1), x))

    def take(n, f, h):
        turn = turned(cflip[n], cback)
        a, b = unpack(CR[n, f, h])
        return turn(a), turn(b)

    def csweep(s, q, i):
        v = CU[s, q, i, CIN]
        total = (CU[s, q, i, CUP] + CU[s, q, i, CDN]) + (CU[s, q, i + 1, CIN] + CU[s, q, i - 1, CIN])
        CU[1 - s, q, i, CIN] = A * v + B * (total + (lo2(v) + hi2(v))) + CC[q, i]

    def cdiverge(s, i):
        v = CU[s, 2, i, CIN]
        return 0.25 * ((CU[s, 0, i, CUP] - CU[s, 0, i, CDN]) + (CU[s, 1, i + 1, CIN] - CU[s, 1, i - 1, CIN])
                       + csgn[i] * (hi2(v) - lo2(v)))

    for q in range(3):
        for copy in ex[q]:
            copy.wait_recv()
        for n, base in ((0, -4), (3, 4), (1, -8), (4, 8)):
            for h in range(2):
                I = C0 + base + 2 * h
                for o, v in zip((I, I + 1), take(n, q, h)):
                    CU[0, q, o, CIN] = v
                    CC[q, o] = v
        CU[0, q, 0, CIN] = take(2, q, 1)[1]
        CU[0, q, 21, CIN] = take(5, q, 0)[0]
        rows(1, 21, lambda i: csweep(0, q, i))
        rows(2, 20, lambda i: csweep(1, q, i))

    for copy in ex[3]:
        copy.wait_recv()
    for n, I, h in ((0, -4, 0), (0, -2, 1), (3, 4, 0), (3, 6, 1), (1, -6, 1), (4, 8, 0)):
        for f, ref in ((3, CE), (4, CG)):
            ref[C0 + I], ref[C0 + I + 1] = take(n, f, h)

    def cpress1(i):
        CP[i, CIN] = -TAU * CE[i] * (cdiverge(0, i) + CG[i])

    rows(3, 19, cpress1)

    def cfirst(i):
        v = CP[i, CIN]
        scale = (-B) / CE[i]
        CC[0, i] = CC[0, i] + scale * (CP[i, CUP] - CP[i, CDN])
        CC[1, i] = CC[1, i] + scale * (CP[i + 1, CIN] - CP[i - 1, CIN])
        CC[2, i] = CC[2, i] + scale * (csgn[i] * (hi2(v) - lo2(v)))
        for q in range(3):
            csweep(0, q, i)

    rows(4, 18, cfirst)
    for q in range(3):
        rows(5, 17, lambda i: csweep(1, q, i))
    for q in range(3):
        rows(6, 16, lambda i: csweep(0, q, i))

    def spread(f, m, v):
        X[f, m, pl.ds(0, 8, stride=2)] = v
        X[f, m, pl.ds(1, 8, stride=2)] = v

    def back_up_p(i):
        spread(3, i - 7, CP[i, CIN] - TAU * CE[i] * (cdiverge(1, i) + CG[i]))

    rows(7, 15, back_up_p)
    turns = (turned(flip_l, back), turned(flip_r, back))
    for copy in halo[3]:
        copy.wait_recv()
    for side, prow in ((0, 4), (1, 17)):
        for n in range(3):
            PB[prow + n, IN] = turns[side](HP_R[side, n])

    def add_p(m):
        for n in range(2):
            PF[4 + 2 * m + n, IN] = PB[4 + 2 * m + n, IN] + X[3, m]

    rows(0, 8, add_p)
    rows(5, 19, lambda i: push(PF, KB[i], i))

    mine = pl.ds(pl.multiple_of(r * 8, 8), 8)

    def place(f):
        return uo_ref.at[f] if f < 3 else po_ref

    def home(f, step):
        rt = lax.rem(r + step, 4)
        return remote(OUT.at[f, pl.ds(4 * rt, 4)], place(f).at[:, mine], os_.at[f, step], or_.at[f], (g, d, rt))

    def own(f):
        return pltpu.make_async_copy(OUT.at[f, layers], place(f).at[:, mine], ol.at[f])

    def send_home(f):
        for step in (2, 1, 3):
            home(f, step).start()
        own(f).start()

    for q in range(3):
        for copy in halo[q]:
            copy.wait_recv()
        for side, urow in ((0, 4), (1, 18)):
            for n in range(2):
                U[1, q, urow + n, IN] = turns[side](HU_R[side, q, n])
        rows(7, 15, lambda i: spread(q, i - 7, CU[1, q, i, CIN]))

        def add_u(m):
            for n in range(2):
                U[0, q, 4 + 2 * m + n, IN] = U[1, q, 4 + 2 * m + n, IN] + X[q, m]

        rows(0, 8, add_u)
        for copy in halo[q]:
            copy.wait_send()
        rows(5, 19, lambda i: sweep(0, q, i))
        rows(6, 18, lambda i: sweep(1, q, i))
        rows(7, 17, lambda i: sweep(0, q, i))
        rows(0, 8, lambda a: set_column(OUT.at[q], a, U[1, q, R0 + a, IN]))
        send_home(q)

    def finish_p(a):
        i = R0 + a
        set_column(OUT.at[3], a, PF[i, IN] - TAU * EB[i] * diverge(1, i, 1.0))

    rows(0, 8, finish_p)
    send_home(3)

    def finish_t(a):
        i = R0 + a
        t = TB[i, IN]
        up, dn, nx, pv, hi, lo = TB[i, UP], TB[i, DN], TB[i + 1, IN], TB[i - 1, IN], hi1(t), lo1(t)
        lap = 6.0 * t - (((up + dn) + (nx + pv)) + (hi + lo))
        carried = 0.5 * (U[1, 0, i, IN] * (up - dn) + U[1, 1, i, IN] * (nx - pv) + U[1, 2, i, IN] * (hi - lo))
        set_column(to_ref, a, t + TIME_STEP * (-KAPPA * lap - carried))

    rows(0, 8, finish_t)

    for copy in halo[3]:
        copy.wait_send()
    for copy in heat:
        copy.wait_send()
    for n in range(5):
        for copy in lateral(n):
            copy.wait_send()
    for group in ex:
        for copy in group:
            copy.wait_send()
    for rt in range(4):
        @pl.when(r != rt)
        def _():
            for n in range(5):
                across(n, rt).wait_send()
    for f in range(4):
        for step in (2, 1, 3):
            home(f, step).wait_send()
        own(f).wait()
    for f in range(4):
        landed(place(f).at[:, pl.ds(0, 24)], or_.at[f])


def write_out(*refs):
    sem = refs[6]
    copies = [pltpu.make_async_copy(refs[n], refs[3 + n], sem.at[n]) for n in range(3)]
    for copy in copies:
        copy.start()
    for copy in copies:
        copy.wait()


def per_device(n_dia, n_chain, t, u, p, e, flags):
    f32 = jnp.float32
    V = pltpu.VMEM
    DMA = pltpu.SemaphoreType.DMA
    any_ = pl.BlockSpec(memory_space=pl.ANY)
    vmem = pl.BlockSpec(memory_space=pltpu.VMEM)
    done = pl.pallas_call(
        functools.partial(kernel, n_dia, n_chain, flags.shape[0]),
        out_shape=(
            V(u.shape, f32),
            V(p.shape, f32),
            V(t.shape, f32),
        ),
        in_specs=[any_] * 5,
        out_specs=(vmem,) * 3,
        scratch_shapes=[
            V((3, 16, 24, 128), f32), V((16, 24, 128), f32), V((16, 24, 128), f32), V((16, 24, 128), f32),
            V((2, 3, 24, 32, 128), f32), V((24, 32, 128), f32), V((24, 32, 128), f32),
            V((24, 16, 128), f32), V((24, 16, 128), f32), V((24, 32, 128), f32),
            V((3, 24, 16, 128), f32), V((24, 16, 128), f32), V((5, 4, 16, 128), f32),
            V((5, 2, 8, 128), f32), V((6, 5, 2, 8, 128), f32),
            V((2, 3, 22, 24, 128), f32), V((3, 22, 8, 128), f32), V((22, 8, 128), f32), V((22, 8, 128), f32),
            V((22, 24, 128), f32), V((4, 8, 16, 128), f32),
            V((2, 3, 2, 16, 128), f32), V((2, 3, 16, 128), f32),
            V((4, 16, 8, 128), f32),
            pltpu.SMEM(flags.shape, jnp.int32), pltpu.SMEM((24,), f32), pltpu.SMEM((22,), f32), pltpu.SMEM((6,), jnp.int32),
            DMA((6, 6)), DMA((11,)), DMA((6,)), DMA((8,)), DMA((8,)), DMA((4, 6)), DMA((4, 6)),
            DMA((4, 4)), DMA((4,)), DMA((4,)), DMA,
        ],
        compiler_params=pltpu.CompilerParams(collective_id=0, has_side_effects=True),
        name="cycle",
    )(t, u, p, e, flags)
    return pl.pallas_call(
        write_out,
        out_shape=[jax.ShapeDtypeStruct(x.shape, f32) for x in done],
        in_specs=[vmem] * 3,
        out_specs=[any_] * 3,
        scratch_shapes=[DMA((3,))],
        name="write_out",
    )(*[pltpu.with_memory_space_constraint(x, pltpu.VMEM) for x in done])


def solution(mesh):
    n_dia = mesh.shape["dia"]
    n_chain = n_dia * mesh.shape["grp"] * mesh.shape["rad"]
    return jax.shard_map(
        functools.partial(per_device, n_dia, n_chain),
        mesh=mesh,
        in_specs=(
            P(None, ("grp", "dia", "rad"), None),
            P(None, "rad", ("grp", "dia"), None),
            P("rad", ("grp", "dia"), None),
            P("rad", ("grp", "dia"), None),
            P(),
        ),
        out_specs=(
            P(None, "rad", ("grp", "dia"), None),
            P("rad", ("grp", "dia"), None),
            P(None, ("grp", "dia", "rad"), None),
        ),
        check_vma=False,
    )
```

```python
import functools

import jax
import jax.numpy as jnp
from jax import lax
from jax.experimental import pallas as pl
from jax.experimental.pallas import tpu as pltpu
from jax.sharding import PartitionSpec as P

DIA_ROWS = 128
OMEGA = 0.8
TAU = 0.25
RAYLEIGH = 4.0
KAPPA = 1.0
TIME_STEP = 0.1
MESH = pl.DeviceIdType.MESH

R0 = 8
HU = 5
HE = 4
IN = pl.ds(8, 16)
UP = pl.ds(9, 16)
DN = pl.ds(7, 16)
CIN = pl.ds(8, 8)
CUP = pl.ds(9, 8)
CDN = pl.ds(7, 8)
C0 = 9
A = 1.0 - OMEGA
B = OMEGA / 6.0


def rows(lo, hi, body, unroll=None):
    unroll = hi - lo if unroll is None else unroll
    lax.fori_loop(lo, hi, lambda i, c: (body(i), c)[1], 0, unroll=unroll)


def column(ref, i):
    layers, width, lanes = ref.shape
    return ref.reshape(layers * width, lanes)[pl.ds(i, layers, stride=width)]


def set_column(ref, i, v):
    layers, width, lanes = ref.shape
    ref.reshape(layers * width, lanes)[pl.ds(i, layers, stride=width)] = v


def span(rt, halo):
    lo, hi = max(0, 8 * rt - halo), min(32, 8 * rt + 8 + halo)
    return lo, hi - lo, lo - 8 * rt + R0


def kernel(
    n_dia, n_chain, n_diamonds,
    t_ref, u_ref, p_ref, e_ref, flag_hbm,
    uo_ref, po_ref, to_ref,
    rawu, rawp, rawe, rawt,
    U, PB, PF, EB, KB, TB, CB, DB, TMP,
    CS, CR, CU, CC, CE, CG, CP, X, HU_R, HP_R, OUT,
    flag_ref, sgn, csgn, cflip,
    gs, gr, ls, hs, hr, xs, xr, os_, or_, ol, fs,
):
    g = lax.axis_index("grp")
    d = lax.axis_index("dia")
    r = lax.axis_index("rad")
    k = g * n_dia + d
    c = k * 4 + r
    n_k = n_chain // 4

    def dev(ci):
        kk = lax.div(ci, 4)
        return (lax.div(kk, n_dia), lax.rem(kk, n_dia), lax.rem(ci, 4))

    def chain(step):
        return dev(lax.rem(c + step + n_chain, n_chain))

    barrier = pltpu.get_barrier_semaphore()
    for step in (1, -1, 2, -2, 3, -3, 4, -4):
        pl.semaphore_signal(barrier, inc=1, device_id=chain(step), device_id_type=MESH)

    pl.semaphore_wait(barrier, 8)

    layers = pl.ds(r * 4, 4)
    srcs = ((p_ref, rawp, HU), (e_ref, rawe, HE)) + tuple((u_ref.at[q], rawu.at[q], HU) for q in range(3))

    def cut(ref, lay, start, size):
        return ref.at[lay, pl.ds(start, size)]

    def remote(src, dst, ssem, rsem, to):
        return pltpu.make_async_remote_copy(
            src_ref=src, dst_ref=dst, send_sem=ssem, recv_sem=rsem, device_id=to, device_id_type=MESH)

    nxt = lax.rem(k + 1, n_k)
    prv = lax.rem(k - 1 + n_k, n_k)
    to_next = (lax.div(nxt, n_dia), lax.rem(nxt, n_dia), 0)
    to_prev = (lax.div(prv, n_dia), lax.rem(prv, n_dia), 3)

    def lateral(n):
        src, dst, halo = srcs[n]
        return [
            remote(cut(src, slice(None), 32 - halo, halo), cut(dst, layers, R0 - halo, halo),
                   gs.at[n, 4], gr.at[5 + n], to_next),
            remote(cut(src, slice(None), 0, halo), cut(dst, layers, R0 + 8, halo),
                   gs.at[n, 5], gr.at[5 + n], to_prev)]

    def across(n, rt):
        src, dst, halo = srcs[n]
        lo, size, at = span(rt, halo)
        return remote(cut(src, slice(None), lo, size), cut(dst, layers, at, size), gs.at[n, rt], gr.at[n], (g, d, rt))

    heat = [
        remote(t_ref.at[:, pl.ds(8 - HE, HE)], rawt.at[:, pl.ds(R0 - HE, HE)], gs.at[5, 0], gr.at[10], chain(1)),
        remote(t_ref.at[:, pl.ds(0, HE)], rawt.at[:, pl.ds(R0 + 8, HE)], gs.at[5, 1], gr.at[10], chain(-1))]
    for rs in range(4):
        @pl.when(r == rs)
        def _():
            for copy in heat:
                copy.start()
            for n in range(5):
                for copy in lateral(n):
                    copy.start()
            for n in range(5):
                for step in (2, 1, 3):
                    across(n, (rs + step) % 4).start()

    read_flags = pltpu.make_async_copy(flag_hbm, flag_ref, fs)
    read_flags.start()
    for rt in range(4):
        @pl.when(r == rt)
        def _():
            for n, (src, dst, halo) in enumerate(srcs):
                lo, size, at = span(rt, halo)
                pltpu.make_async_copy(cut(src, slice(None), lo, size), cut(dst, layers, at, size), ls.at[n]).start()
    pltpu.make_async_copy(t_ref, rawt.at[:, pl.ds(R0, 8)], ls.at[5]).start()

    z = jnp.zeros((8, 128), jnp.float32)

    def clear(i):
        for s in range(2):
            for q in range(3):
                U[s, q, i, pl.ds(0, 8)] = z
                U[s, q, i, pl.ds(24, 8)] = z
        for ref in (PB, PF, TB):
            ref[i, pl.ds(0, 8)] = z
            ref[i, pl.ds(24, 8)] = z

    rows(0, 24, clear, 1)

    def cclear(i):
        for s in range(2):
            for q in range(3):
                CU[s, q, i, pl.ds(0, 8)] = z
                CU[s, q, i, pl.ds(16, 8)] = z
        CP[i, pl.ds(0, 8)] = z
        CP[i, pl.ds(16, 8)] = z

    rows(0, 22, cclear, 1)

    read_flags.wait()
    per = DIA_ROWS // 32
    left = jnp.where((lax.rem(k, per) == 0) & (flag_ref[lax.div(k, per)] == 1), 1, 0)
    right = jnp.where(
        (lax.rem(k + 1, per) == 0) & (flag_ref[lax.rem(lax.div(k + 1, per), n_diamonds)] == 1), 1, 0)

    def flip_of(j, width, block):
        return jnp.where(j < -width * r, left, jnp.where(j >= block - width * r, right, 0))

    for i in range(24):
        sgn[i] = jnp.where(flip_of(i - R0, 8, 32) == 1, -1.0, 1.0)
    for i in range(22):
        csgn[i] = jnp.where(flip_of(i - C0, 4, 16) == 1, -1.0, 1.0)
    for n, J in enumerate((-4, -8, -12, 4, 8, 12)):
        cflip[n] = flip_of(J, 4, 16)
    flip_l, flip_r = flip_of(-1, 8, 32), flip_of(8, 8, 32)

    lane = lax.broadcasted_iota(jnp.int32, (16, 128), 1)
    clane = lax.broadcasted_iota(jnp.int32, (8, 128), 1)
    even = lax.rem(clane, 2) == 0
    back = 127 - lane
    cback = 127 - clane

    def lo1(v):
        return jnp.where(lane == 0, 0.0, pltpu.roll(v, 1, 1))

    def hi1(v):
        return jnp.where(lane == 127, 0.0, pltpu.roll(v, 127, 1))

    def lo2(v):
        return jnp.where(clane < 2, 0.0, pltpu.roll(v, 2, 1))

    def hi2(v):
        return jnp.where(clane >= 126, 0.0, pltpu.roll(v, 126, 1))

    def landed(ref, sem):
        pltpu.make_async_copy(ref, ref, sem).wait()

    def gathered(which):
        for rt in range(4):
            @pl.when(r == rt)
            def _():
                for n in which:
                    src, dst, halo = srcs[n]
                    lo, size, at = span(rt, halo)
                    landed(cut(dst, slice(0, 4), at, size), ls.at[n])
                    landed(cut(dst, slice(0, 12), at, size), gr.at[n])
                    if rt in (0, 3):
                        landed(cut(dst, slice(0, 16), at, halo), gr.at[5 + n])

    gathered((0, 1))
    landed(rawt.at[:, pl.ds(R0, 8)], ls.at[5])
    landed(rawt.at[:, pl.ds(R0, 2 * HE)], gr.at[10])

    def put_scalars(i, turn):
        PB[i, IN] = turn(column(rawp, i))
        EB[i] = turn(column(rawe, i))
        TB[i, IN] = turn(column(rawt, i))

    def put_vector(q, i, turn):
        U[0, q, i, IN] = turn(column(rawu.at[q], i))

    def turned(flag, idx):
        return lambda v: jnp.where(flag == 1, jnp.take_along_axis(v, idx, axis=1), v)

    def put_all(put):
        rows(8, 16, lambda i: put(i, lambda v: v))
        rows(R0 - HU, R0, lambda i: put(i, turned(flip_l, back)))
        rows(R0 + 8, R0 + 8 + HU, lambda i: put(i, turned(flip_r, back)))

    put_all(put_scalars)

    def stencil(ref, s, q, i):
        v = ref[s, q, i, IN]
        total = (ref[s, q, i, UP] + ref[s, q, i, DN]) + (ref[s, q, i + 1, IN] + ref[s, q, i - 1, IN])
        return v, total + (lo1(v) + hi1(v))

    def sweep(s, q, i):
        v, total = stencil(U, s, q, i)
        U[1 - s, q, i, IN] = A * v + B * total + CB[q, i]

    def slope(ref, i, sign):
        v = ref[i, IN]
        return (ref[i, UP] - ref[i, DN], ref[i + 1, IN] - ref[i - 1, IN], sign * (hi1(v) - lo1(v)))

    def diverge(s, i, sign):
        v = U[s, 2, i, IN]
        return 0.5 * ((U[s, 0, i, UP] - U[s, 0, i, DN]) + (U[s, 1, i + 1, IN] - U[s, 1, i - 1, IN])
                      + sign * (hi1(v) - lo1(v)))

    def push(press, kinv, i):
        gr_, ga_, gb_ = slope(press, i, sgn[i])
        half = -0.5 * kinv
        CB[0, i] = kinv * (RAYLEIGH * TB[i, IN]) + half * gr_
        CB[1, i] = half * ga_
        CB[2, i] = half * gb_

    def first_push(i):
        kinv = B / EB[i]
        KB[i] = kinv
        push(PB, kinv, i)

    rows(4, 20, first_push)
    for q in range(3):
        gathered((2 + q,))
        put_all(functools.partial(put_vector, q))
        rows(4, 20, lambda i: sweep(0, q, i))
        rows(5, 19, lambda i: sweep(1, q, i))
        rows(6, 18, lambda i: sweep(0, q, i))

    halo = []
    for q in range(3):
        halo.append((remote(U.at[1, q, pl.ds(R0 + 4, 2), IN], HU_R.at[0, q], hs.at[2 * q], hr.at[2 * q], chain(1)),
                     remote(U.at[1, q, pl.ds(R0 + 2, 2), IN], HU_R.at[1, q], hs.at[2 * q + 1], hr.at[2 * q + 1], chain(-1))))
    halo.append((remote(PB.at[pl.ds(R0 + 4, 3), IN], HP_R.at[0], hs.at[6], hr.at[6], chain(1)),
                 remote(PB.at[pl.ds(R0 + 1, 3), IN], HP_R.at[1], hs.at[7], hr.at[7], chain(-1))))

    def pre_pressure(i):
        div = diverge(1, i, sgn[i])
        DB[i] = div
        PB[i, IN] = PB[i, IN] - TAU * EB[i] * div

    rows(7, 17, pre_pressure)
    for copy in halo[3]:
        copy.start()

    def restrict(f, m, acc):
        TMP[f, m] = acc
        v = TMP[f, m, pl.ds(0, 8, stride=2)] + TMP[f, m, pl.ds(1, 8, stride=2)]
        return 0.125 * (v + jnp.where(even, pltpu.roll(v, 127, 1), pltpu.roll(v, 1, 1)))

    def pack(f, vals):
        for h in range(2):
            CS[f, h] = jnp.where(even, vals[2 * h], vals[2 * h + 1])

    def residual(q, ii):
        v, total = stencil(U, 1, q, ii)
        w = PB[ii, IN]
        if q == 0:
            gp = PB[ii, UP] - PB[ii, DN]
        elif q == 1:
            gp = PB[ii + 1, IN] - PB[ii - 1, IN]
        else:
            gp = hi1(w) - lo1(w)
        res = -0.5 * gp - EB[ii] * (6.0 * v - total)
        return res + RAYLEIGH * TB[ii, IN] if q == 0 else res

    def send_vector(q):
        one = pl.ds(q, 1)
        out = [
            remote(CS.at[one], CR.at[1, one], xs.at[q, 1], xr.at[q, 1], chain(2)),
            remote(CS.at[one], CR.at[4, one], xs.at[q, 4], xr.at[q, 4], chain(-2)),
            remote(CS.at[one, pl.ds(1, 1)], CR.at[2, one, pl.ds(1, 1)], xs.at[q, 2], xr.at[q, 2], chain(3)),
            remote(CS.at[one, pl.ds(0, 1)], CR.at[5, one, pl.ds(0, 1)], xs.at[q, 5], xr.at[q, 5], chain(-3)),
            remote(CS.at[one], CR.at[0, one], xs.at[q, 0], xr.at[q, 0], chain(1)),
            remote(CS.at[one], CR.at[3, one], xs.at[q, 3], xr.at[q, 3], chain(-1)),
        ]
        for copy in out:
            copy.start()
        return out

    ce = [restrict(3, m, EB[R0 + 2 * m] + EB[R0 + 2 * m + 1]) for m in range(4)]
    cg = [restrict(4, m, DB[R0 + 2 * m] + DB[R0 + 2 * m + 1]) for m in range(4)]
    cinv = [(4.0 * B) / e for e in ce]
    ex = []
    for q in range(3):
        vals = [cinv[m] * restrict(q, m, residual(q, R0 + 2 * m) + residual(q, R0 + 2 * m + 1)) for m in range(4)]
        pack(q, vals)
        ex.append(send_vector(q))
        for m in range(4):
            CU[0, q, C0 + m, CIN] = vals[m]
            CC[q, C0 + m] = vals[m]
    pack(3, ce)
    pack(4, cg)
    both = pl.ds(3, 2)
    ex.append([
        remote(CS.at[both, pl.ds(1, 1)], CR.at[1, both, pl.ds(1, 1)], xs.at[3, 1], xr.at[3, 1], chain(2)),
        remote(CS.at[both, pl.ds(0, 1)], CR.at[4, both, pl.ds(0, 1)], xs.at[3, 4], xr.at[3, 4], chain(-2)),
        remote(CS.at[both], CR.at[0, both], xs.at[3, 0], xr.at[3, 0], chain(1)),
        remote(CS.at[both], CR.at[3, both], xs.at[3, 3], xr.at[3, 3], chain(-1)),
    ])
    for copy in ex[3]:
        copy.start()
    for pair in halo[:3]:
        for copy in pair:
            copy.start()
    for m in range(4):
        CE[C0 + m] = ce[m]
        CG[C0 + m] = cg[m]

    def unpack(x):
        return (jnp.where(even, x, pltpu.roll(x, 1, 1)), jnp.where(even, pltpu.roll(x, 127, 1), x))

    def take(n, f, h):
        turn = turned(cflip[n], cback)
        a, b = unpack(CR[n, f, h])
        return turn(a), turn(b)

    def csweep(s, q, i):
        v = CU[s, q, i, CIN]
        total = (CU[s, q, i, CUP] + CU[s, q, i, CDN]) + (CU[s, q, i + 1, CIN] + CU[s, q, i - 1, CIN])
        CU[1 - s, q, i, CIN] = A * v + B * (total + (lo2(v) + hi2(v))) + CC[q, i]

    def cdiverge(s, i):
        v = CU[s, 2, i, CIN]
        return 0.25 * ((CU[s, 0, i, CUP] - CU[s, 0, i, CDN]) + (CU[s, 1, i + 1, CIN] - CU[s, 1, i - 1, CIN])
                       + csgn[i] * (hi2(v) - lo2(v)))

    for q in range(3):
        for copy in ex[q]:
            copy.wait_recv()
        for n, base in ((0, -4), (3, 4), (1, -8), (4, 8)):
            for h in range(2):
                I = C0 + base + 2 * h
                for o, v in zip((I, I + 1), take(n, q, h)):
                    CU[0, q, o, CIN] = v
                    CC[q, o] = v
        CU[0, q, 0, CIN] = take(2, q, 1)[1]
        CU[0, q, 21, CIN] = take(5, q, 0)[0]
        rows(1, 21, lambda i: csweep(0, q, i))
        rows(2, 20, lambda i: csweep(1, q, i))

    for copy in ex[3]:
        copy.wait_recv()
    for n, I, h in ((0, -4, 0), (0, -2, 1), (3, 4, 0), (3, 6, 1), (1, -6, 1), (4, 8, 0)):
        for f, ref in ((3, CE), (4, CG)):
            ref[C0 + I], ref[C0 + I + 1] = take(n, f, h)

    def cpress1(i):
        CP[i, CIN] = -TAU * CE[i] * (cdiverge(0, i) + CG[i])

    rows(3, 19, cpress1)

    def cfirst(i):
        v = CP[i, CIN]
        scale = (-B) / CE[i]
        CC[0, i] = CC[0, i] + scale * (CP[i, CUP] - CP[i, CDN])
        CC[1, i] = CC[1, i] + scale * (CP[i + 1, CIN] - CP[i - 1, CIN])
        CC[2, i] = CC[2, i] + scale * (csgn[i] * (hi2(v) - lo2(v)))
        for q in range(3):
            csweep(0, q, i)

    rows(4, 18, cfirst)
    for q in range(3):
        rows(5, 17, lambda i: csweep(1, q, i))
    for q in range(3):
        rows(6, 16, lambda i: csweep(0, q, i))

    def spread(f, m, v):
        X[f, m, pl.ds(0, 8, stride=2)] = v
        X[f, m, pl.ds(1, 8, stride=2)] = v

    def back_up_p(i):
        spread(3, i - 7, CP[i, CIN] - TAU * CE[i] * (cdiverge(1, i) + CG[i]))

    rows(7, 15, back_up_p)
    turns = (turned(flip_l, back), turned(flip_r, back))
    for copy in halo[3]:
        copy.wait_recv()
    for side, prow in ((0, 4), (1, 17)):
        for n in range(3):
            PB[prow + n, IN] = turns[side](HP_R[side, n])

    def add_p(m):
        for n in range(2):
            PF[4 + 2 * m + n, IN] = PB[4 + 2 * m + n, IN] + X[3, m]

    rows(0, 8, add_p)
    rows(5, 19, lambda i: push(PF, KB[i], i))

    mine = pl.ds(pl.multiple_of(r * 8, 8), 8)

    def place(f):
        return uo_ref.at[f] if f < 3 else po_ref

    def home(f, step):
        rt = lax.rem(r + step, 4)
        return remote(OUT.at[f, pl.ds(4 * rt, 4)], place(f).at[:, mine], os_.at[f, step], or_.at[f], (g, d, rt))

    def own(f):
        return pltpu.make_async_copy(OUT.at[f, layers], place(f).at[:, mine], ol.at[f])

    def send_home(f):
        for step in (2, 1, 3):
            home(f, step).start()
        own(f).start()

    for q in range(3):
        for copy in halo[q]:
            copy.wait_recv()
        for side, urow in ((0, 4), (1, 18)):
            for n in range(2):
                U[1, q, urow + n, IN] = turns[side](HU_R[side, q, n])
        rows(7, 15, lambda i: spread(q, i - 7, CU[1, q, i, CIN]))

        def add_u(m):
            for n in range(2):
                U[0, q, 4 + 2 * m + n, IN] = U[1, q, 4 + 2 * m + n, IN] + X[q, m]

        rows(0, 8, add_u)
        for copy in halo[q]:
            copy.wait_send()
        rows(5, 19, lambda i: sweep(0, q, i))
        rows(6, 18, lambda i: sweep(1, q, i))
        rows(7, 17, lambda i: sweep(0, q, i))
        rows(0, 8, lambda a: set_column(OUT.at[q], a, U[1, q, R0 + a, IN]))
        send_home(q)

    def finish_p(a):
        i = R0 + a
        set_column(OUT.at[3], a, PF[i, IN] - TAU * EB[i] * diverge(1, i, 1.0))

    rows(0, 8, finish_p)
    send_home(3)

    def finish_t(a):
        i = R0 + a
        t = TB[i, IN]
        up, dn, nx, pv, hi, lo = TB[i, UP], TB[i, DN], TB[i + 1, IN], TB[i - 1, IN], hi1(t), lo1(t)
        lap = 6.0 * t - (((up + dn) + (nx + pv)) + (hi + lo))
        carried = 0.5 * (U[1, 0, i, IN] * (up - dn) + U[1, 1, i, IN] * (nx - pv) + U[1, 2, i, IN] * (hi - lo))
        set_column(to_ref, a, t + TIME_STEP * (-KAPPA * lap - carried))

    rows(0, 8, finish_t)

    for copy in halo[3]:
        copy.wait_send()
    for copy in heat:
        copy.wait_send()
    for n in range(5):
        for copy in lateral(n):
            copy.wait_send()
    for group in ex:
        for copy in group:
            copy.wait_send()
    for rt in range(4):
        @pl.when(r != rt)
        def _():
            for n in range(5):
                across(n, rt).wait_send()
    for f in range(4):
        for step in (2, 1, 3):
            home(f, step).wait_send()
        own(f).wait()
    for f in range(4):
        landed(place(f).at[:, pl.ds(0, 24)], or_.at[f])


def write_out(*refs):
    sem = refs[6]
    copies = [pltpu.make_async_copy(refs[n], refs[3 + n], sem.at[n]) for n in range(3)]
    for copy in copies:
        copy.start()
    for copy in copies:
        copy.wait()


def per_device(n_dia, n_chain, t, u, p, e, flags):
    f32 = jnp.float32
    V = pltpu.VMEM
    DMA = pltpu.SemaphoreType.DMA
    any_ = pl.BlockSpec(memory_space=pl.ANY)
    vmem = pl.BlockSpec(memory_space=pltpu.VMEM)
    done = pl.pallas_call(
        functools.partial(kernel, n_dia, n_chain, flags.shape[0]),
        out_shape=(
            V(u.shape, f32),
            V(p.shape, f32),
            V(t.shape, f32),
        ),
        in_specs=[any_] * 5,
        out_specs=(vmem,) * 3,
        scratch_shapes=[
            V((3, 16, 24, 128), f32), V((16, 24, 128), f32), V((16, 24, 128), f32), V((16, 24, 128), f32),
            V((2, 3, 24, 32, 128), f32), V((24, 32, 128), f32), V((24, 32, 128), f32),
            V((24, 16, 128), f32), V((24, 16, 128), f32), V((24, 32, 128), f32),
            V((3, 24, 16, 128), f32), V((24, 16, 128), f32), V((5, 4, 16, 128), f32),
            V((5, 2, 8, 128), f32), V((6, 5, 2, 8, 128), f32),
            V((2, 3, 22, 24, 128), f32), V((3, 22, 8, 128), f32), V((22, 8, 128), f32), V((22, 8, 128), f32),
            V((22, 24, 128), f32), V((4, 8, 16, 128), f32),
            V((2, 3, 2, 16, 128), f32), V((2, 3, 16, 128), f32),
            V((4, 16, 8, 128), f32),
            pltpu.SMEM(flags.shape, jnp.int32), pltpu.SMEM((24,), f32), pltpu.SMEM((22,), f32), pltpu.SMEM((6,), jnp.int32),
            DMA((6, 6)), DMA((11,)), DMA((6,)), DMA((8,)), DMA((8,)), DMA((4, 6)), DMA((4, 6)),
            DMA((4, 4)), DMA((4,)), DMA((4,)), DMA,
        ],
        compiler_params=pltpu.CompilerParams(collective_id=0, has_side_effects=True),
        name="cycle",
    )(t, u, p, e, flags)
    return pl.pallas_call(
        write_out,
        out_shape=[jax.ShapeDtypeStruct(x.shape, f32) for x in done],
        in_specs=[vmem] * 3,
        out_specs=[any_] * 3,
        scratch_shapes=[DMA((3,))],
        name="write_out",
    )(*[pltpu.with_memory_space_constraint(x, pltpu.VMEM) for x in done])


def solution(mesh):
    n_dia = mesh.shape["dia"]
    n_chain = n_dia * mesh.shape["grp"] * mesh.shape["rad"]
    return jax.shard_map(
        functools.partial(per_device, n_dia, n_chain),
        mesh=mesh,
        in_specs=(
            P(None, ("grp", "dia", "rad"), None),
            P(None, "rad", ("grp", "dia"), None),
            P("rad", ("grp", "dia"), None),
            P("rad", ("grp", "dia"), None),
            P(),
        ),
        out_specs=(
            P(None, "rad", ("grp", "dia"), None),
            P("rad", ("grp", "dia"), None),
            P(None, ("grp", "dia", "rad"), None),
        ),
        check_vma=False,
    )
```

```python
import functools

import jax
import jax.numpy as jnp
from jax import lax
from jax.experimental import pallas as pl
from jax.experimental.pallas import tpu as pltpu
from jax.sharding import PartitionSpec as P

DIA_ROWS = 128
OMEGA = 0.8
TAU = 0.25
RAYLEIGH = 4.0
KAPPA = 1.0
TIME_STEP = 0.1
MESH = pl.DeviceIdType.MESH

R0 = 8
HU = 5
HE = 4
IN = pl.ds(8, 16)
UP = pl.ds(9, 16)
DN = pl.ds(7, 16)
CIN = pl.ds(8, 8)
CUP = pl.ds(9, 8)
CDN = pl.ds(7, 8)
C0 = 9
A = 1.0 - OMEGA
B = OMEGA / 6.0


def rows(lo, hi, body, unroll=None):
    unroll = hi - lo if unroll is None else unroll
    lax.fori_loop(lo, hi, lambda i, c: (body(i), c)[1], 0, unroll=unroll)


def column(ref, i):
    layers, width, lanes = ref.shape
    return ref.reshape(layers * width, lanes)[pl.ds(i, layers, stride=width)]


def set_column(ref, i, v):
    layers, width, lanes = ref.shape
    ref.reshape(layers * width, lanes)[pl.ds(i, layers, stride=width)] = v


def span(rt, halo):
    lo, hi = max(0, 8 * rt - halo), min(32, 8 * rt + 8 + halo)
    return lo, hi - lo, lo - 8 * rt + R0


def kernel(
    n_dia, n_chain, n_diamonds,
    t_ref, u_ref, p_ref, e_ref, flag_hbm,
    uo_ref, po_ref, to_ref,
    rawu, rawp, rawe, rawt,
    U, PB, PF, EB, KB, TB, CB, DB, TMP,
    CS, CR, CU, CC, CE, CG, CP, X, HU_R, HP_R, OUT,
    flag_ref, sgn, csgn, cflip,
    gs, gr, ls, hs, hr, xs, xr, os_, or_, ol, fs, go,
):
    g = lax.axis_index("grp")
    d = lax.axis_index("dia")
    r = lax.axis_index("rad")
    k = g * n_dia + d
    n_k = n_chain // 4
    n_grp = n_k // n_dia

    over = d == n_dia - 1
    under = d == 0
    next_g = jnp.where(over, jnp.where(g == n_grp - 1, 0, g + 1), g)
    next_d = jnp.where(over, 0, d + 1)
    prev_g = jnp.where(under, jnp.where(g == 0, n_grp - 1, g - 1), g)
    prev_d = jnp.where(under, n_dia - 1, d - 1)
    to_next, to_prev = (next_g, next_d, 0), (prev_g, prev_d, 3)
    chains = {4: (next_g, next_d, r), -4: (prev_g, prev_d, r)}
    for step in (1, 2, 3):
        out = r + step >= 4
        chains[step] = (jnp.where(out, next_g, g), jnp.where(out, next_d, d), jnp.where(out, r + step - 4, r + step))
        out = r - step < 0
        chains[-step] = (jnp.where(out, prev_g, g), jnp.where(out, prev_d, d), jnp.where(out, r - step + 4, r - step))

    def chain(step):
        return chains[step]

    def signal(sem, to):
        pl.semaphore_signal(sem, inc=1, device_id=to, device_id_type=MESH)

    barrier = pltpu.get_barrier_semaphore()
    for step in (1, 2, 3):
        signal(barrier, (g, d, jnp.where(r + step >= 4, r + step - 4, r + step)))
    for step in (1, 2, 3, 4):
        @pl.when(r - step < 0)
        def _():
            signal(barrier, chain(-step))
    pl.semaphore_wait(barrier, r + 4)
    for step in (1, 2, 3, 4):
        @pl.when(r + step >= 4)
        def _():
            signal(go, chain(step))

    layers = pl.ds(r * 4, 4)
    srcs = ((p_ref, rawp, HU), (e_ref, rawe, HE)) + tuple((u_ref.at[q], rawu.at[q], HU) for q in range(3))

    def cut(ref, lay, start, size):
        return ref.at[lay, pl.ds(start, size)]

    def remote(src, dst, ssem, rsem, to):
        return pltpu.make_async_remote_copy(
            src_ref=src, dst_ref=dst, send_sem=ssem, recv_sem=rsem, device_id=to, device_id_type=MESH)

    def lateral(n):
        src, dst, halo = srcs[n]
        return [
            remote(cut(src, slice(None), 32 - halo, halo), cut(dst, layers, R0 - halo, halo),
                   gs.at[n, 4], gr.at[5 + n], to_next),
            remote(cut(src, slice(None), 0, halo), cut(dst, layers, R0 + 8, halo),
                   gs.at[n, 5], gr.at[5 + n], to_prev)]

    def across(n, rt):
        src, dst, halo = srcs[n]
        lo, size, at = span(rt, halo)
        return remote(cut(src, slice(None), lo, size), cut(dst, layers, at, size), gs.at[n, rt], gr.at[n], (g, d, rt))

    heat = [
        remote(t_ref.at[:, pl.ds(8 - HE, HE)], rawt.at[:, pl.ds(R0 - HE, HE)], gs.at[5, 0], gr.at[10], chain(1)),
        remote(t_ref.at[:, pl.ds(0, HE)], rawt.at[:, pl.ds(R0 + 8, HE)], gs.at[5, 1], gr.at[10], chain(-1))]
    def send_across(fields):
        for rs in range(4):
            @pl.when(r == rs)
            def _():
                for n in fields:
                    for step in (2, 1, 3):
                        across(n, (rs + step) % 4).start()

    heat[0].start()
    for n in range(5):
        lateral(n)[0].start()
    send_across((0, 1))

    read_flags = pltpu.make_async_copy(flag_hbm, flag_ref, fs)
    read_flags.start()
    for rt in range(4):
        @pl.when(r == rt)
        def _():
            for n, (src, dst, halo) in enumerate(srcs):
                lo, size, at = span(rt, halo)
                pltpu.make_async_copy(cut(src, slice(None), lo, size), cut(dst, layers, at, size), ls.at[n]).start()
    pltpu.make_async_copy(t_ref, rawt.at[:, pl.ds(R0, 8)], ls.at[5]).start()

    z = jnp.zeros((8, 128), jnp.float32)

    def clear(i):
        for s in range(2):
            for q in range(3):
                U[s, q, i, pl.ds(0, 8)] = z
                U[s, q, i, pl.ds(24, 8)] = z
        for ref in (PB, PF, TB):
            ref[i, pl.ds(0, 8)] = z
            ref[i, pl.ds(24, 8)] = z

    rows(0, 24, clear, 1)

    def cclear(i):
        for s in range(2):
            for q in range(3):
                CU[s, q, i, pl.ds(0, 8)] = z
                CU[s, q, i, pl.ds(16, 8)] = z
        CP[i, pl.ds(0, 8)] = z
        CP[i, pl.ds(16, 8)] = z

    rows(0, 22, cclear, 1)
    pl.semaphore_wait(go, 4 - r)
    heat[1].start()
    for n in range(5):
        lateral(n)[1].start()
    send_across((2, 3, 4))

    read_flags.wait()
    per = DIA_ROWS // 32
    left = jnp.where((lax.rem(k, per) == 0) & (flag_ref[lax.div(k, per)] == 1), 1, 0)
    right = jnp.where(
        (lax.rem(k + 1, per) == 0) & (flag_ref[lax.rem(lax.div(k + 1, per), n_diamonds)] == 1), 1, 0)

    def flip_of(j, width, block):
        return jnp.where(j < -width * r, left, jnp.where(j >= block - width * r, right, 0))

    for i in range(24):
        sgn[i] = jnp.where(flip_of(i - R0, 8, 32) == 1, -1.0, 1.0)
    for i in range(22):
        csgn[i] = jnp.where(flip_of(i - C0, 4, 16) == 1, -1.0, 1.0)
    for n, J in enumerate((-4, -8, -12, 4, 8, 12)):
        cflip[n] = flip_of(J, 4, 16)
    flip_l, flip_r = flip_of(-1, 8, 32), flip_of(8, 8, 32)

    lane = lax.broadcasted_iota(jnp.int32, (16, 128), 1)
    clane = lax.broadcasted_iota(jnp.int32, (8, 128), 1)
    even = lax.rem(clane, 2) == 0
    back = 127 - lane
    cback = 127 - clane

    def lo1(v):
        return jnp.where(lane == 0, 0.0, pltpu.roll(v, 1, 1))

    def hi1(v):
        return jnp.where(lane == 127, 0.0, pltpu.roll(v, 127, 1))

    def lo2(v):
        return jnp.where(clane < 2, 0.0, pltpu.roll(v, 2, 1))

    def hi2(v):
        return jnp.where(clane >= 126, 0.0, pltpu.roll(v, 126, 1))

    def landed(ref, sem):
        pltpu.make_async_copy(ref, ref, sem).wait()

    def gathered(which):
        for rt in range(4):
            @pl.when(r == rt)
            def _():
                for n in which:
                    src, dst, halo = srcs[n]
                    lo, size, at = span(rt, halo)
                    landed(cut(dst, slice(0, 4), at, size), ls.at[n])
                    landed(cut(dst, slice(0, 12), at, size), gr.at[n])
                    if rt in (0, 3):
                        landed(cut(dst, slice(0, 16), at, halo), gr.at[5 + n])

    gathered((0, 1))
    landed(rawt.at[:, pl.ds(R0, 8)], ls.at[5])
    landed(rawt.at[:, pl.ds(R0, 2 * HE)], gr.at[10])

    def put_scalars(i, turn):
        PB[i, IN] = turn(column(rawp, i))
        EB[i] = turn(column(rawe, i))
        TB[i, IN] = turn(column(rawt, i))

    def put_vector(q, i, turn):
        U[0, q, i, IN] = turn(column(rawu.at[q], i))

    def turned(flag, idx):
        return lambda v: jnp.where(flag == 1, jnp.take_along_axis(v, idx, axis=1), v)

    def put_all(put):
        rows(8, 16, lambda i: put(i, lambda v: v))
        rows(R0 - HU, R0, lambda i: put(i, turned(flip_l, back)))
        rows(R0 + 8, R0 + 8 + HU, lambda i: put(i, turned(flip_r, back)))

    put_all(put_scalars)

    def stencil(ref, s, q, i):
        v = ref[s, q, i, IN]
        total = (ref[s, q, i, UP] + ref[s, q, i, DN]) + (ref[s, q, i + 1, IN] + ref[s, q, i - 1, IN])
        return v, total + (lo1(v) + hi1(v))

    def sweep(s, q, i):
        v, total = stencil(U, s, q, i)
        U[1 - s, q, i, IN] = A * v + B * total + CB[q, i]

    def diverge(s, i, sign):
        v = U[s, 2, i, IN]
        return 0.5 * ((U[s, 0, i, UP] - U[s, 0, i, DN]) + (U[s, 1, i + 1, IN] - U[s, 1, i - 1, IN])
                      + sign * (hi1(v) - lo1(v)))

    def push(press, kinv, q, i):
        half = -0.5 * kinv
        if q == 0:
            CB[0, i] = kinv * (RAYLEIGH * TB[i, IN]) + half * (press[i, UP] - press[i, DN])
        elif q == 1:
            CB[1, i] = half * (press[i + 1, IN] - press[i - 1, IN])
        else:
            v = press[i, IN]
            CB[2, i] = half * (sgn[i] * (hi1(v) - lo1(v)))

    def first_push(i):
        kinv = B / EB[i]
        KB[i] = kinv
        for q in range(3):
            push(PB, kinv, q, i)

    rows(4, 20, first_push)
    def restrict(f, m, acc):
        TMP[f, m] = acc
        v = TMP[f, m, pl.ds(0, 8, stride=2)] + TMP[f, m, pl.ds(1, 8, stride=2)]
        return 0.125 * (v + jnp.where(even, pltpu.roll(v, 127, 1), pltpu.roll(v, 1, 1)))

    def pack(f, vals):
        for h in range(2):
            CS[f, h] = jnp.where(even, vals[2 * h], vals[2 * h + 1])

    def send_scalar(f):
        one = pl.ds(f, 1)
        out = [
            remote(CS.at[one, pl.ds(1, 1)], CR.at[1, one, pl.ds(1, 1)], xs.at[f, 1], xr.at[f, 1], chain(2)),
            remote(CS.at[one, pl.ds(0, 1)], CR.at[4, one, pl.ds(0, 1)], xs.at[f, 4], xr.at[f, 4], chain(-2)),
            remote(CS.at[one], CR.at[0, one], xs.at[f, 0], xr.at[f, 0], chain(1)),
            remote(CS.at[one], CR.at[3, one], xs.at[f, 3], xr.at[f, 3], chain(-1)),
        ]
        for copy in out:
            copy.start()
        return out

    ce = [restrict(3, m, EB[R0 + 2 * m] + EB[R0 + 2 * m + 1]) for m in range(4)]
    cinv = [(4.0 * B) / e for e in ce]
    pack(3, ce)
    for m in range(4):
        CE[C0 + m] = ce[m]

    for q in range(3):
        gathered((2 + q,))
        if q == 2:
            ex_e = send_scalar(3)
        put_all(functools.partial(put_vector, q))
        rows(4, 20, lambda i: sweep(0, q, i))
        rows(5, 19, lambda i: sweep(1, q, i))
        rows(6, 18, lambda i: sweep(0, q, i))

    halo = []
    for q in range(3):
        halo.append((remote(U.at[1, q, pl.ds(R0 + 4, 2), IN], HU_R.at[0, q], hs.at[2 * q], hr.at[2 * q], chain(1)),
                     remote(U.at[1, q, pl.ds(R0 + 2, 2), IN], HU_R.at[1, q], hs.at[2 * q + 1], hr.at[2 * q + 1], chain(-1))))
    halo.append((remote(PB.at[pl.ds(R0 + 4, 3), IN], HP_R.at[0], hs.at[6], hr.at[6], chain(1)),
                 remote(PB.at[pl.ds(R0 + 1, 3), IN], HP_R.at[1], hs.at[7], hr.at[7], chain(-1))))

    def pre_pressure(i):
        div = diverge(1, i, sgn[i])
        DB[i] = div
        PB[i, IN] = PB[i, IN] - TAU * EB[i] * div

    rows(7, 17, pre_pressure)

    def residual(q, ii):
        v, total = stencil(U, 1, q, ii)
        w = PB[ii, IN]
        if q == 0:
            gp = PB[ii, UP] - PB[ii, DN]
        elif q == 1:
            gp = PB[ii + 1, IN] - PB[ii - 1, IN]
        else:
            gp = hi1(w) - lo1(w)
        res = -0.5 * gp - EB[ii] * (6.0 * v - total)
        return res + RAYLEIGH * TB[ii, IN] if q == 0 else res

    def send_vector(q):
        one = pl.ds(q, 1)
        out = [
            remote(CS.at[one], CR.at[1, one], xs.at[q, 1], xr.at[q, 1], chain(2)),
            remote(CS.at[one, pl.ds(1, 1)], CR.at[2, one, pl.ds(1, 1)], xs.at[q, 2], xr.at[q, 2], chain(3)),
            remote(CS.at[one], CR.at[0, one], xs.at[q, 0], xr.at[q, 0], chain(1)),
            remote(CS.at[one], CR.at[4, one], xs.at[q, 4], xr.at[q, 4], chain(-2)),
            remote(CS.at[one, pl.ds(0, 1)], CR.at[5, one, pl.ds(0, 1)], xs.at[q, 5], xr.at[q, 5], chain(-3)),
            remote(CS.at[one], CR.at[3, one], xs.at[q, 3], xr.at[q, 3], chain(-1)),
        ]
        for copy in out:
            copy.start()
        return out

    ex = []
    for q in range(3):
        vals = [cinv[m] * restrict(q, m, residual(q, R0 + 2 * m) + residual(q, R0 + 2 * m + 1)) for m in range(4)]
        pack(q, vals)
        ex.append(send_vector(q))
        for m in range(4):
            CU[0, q, C0 + m, CIN] = vals[m]
            CC[q, C0 + m] = vals[m]
    cg = [restrict(4, m, DB[R0 + 2 * m] + DB[R0 + 2 * m + 1]) for m in range(4)]
    pack(4, cg)
    ex.append(ex_e + send_scalar(4))
    for pair in (halo[3],) + tuple(halo[:3]):
        for copy in pair:
            copy.start()
    for m in range(4):
        CG[C0 + m] = cg[m]

    def unpack(x):
        return (jnp.where(even, x, pltpu.roll(x, 1, 1)), jnp.where(even, pltpu.roll(x, 127, 1), x))

    def take(n, f, h):
        turn = turned(cflip[n], cback)
        a, b = unpack(CR[n, f, h])
        return turn(a), turn(b)

    def csweep(s, q, i):
        v = CU[s, q, i, CIN]
        total = (CU[s, q, i, CUP] + CU[s, q, i, CDN]) + (CU[s, q, i + 1, CIN] + CU[s, q, i - 1, CIN])
        CU[1 - s, q, i, CIN] = A * v + B * (total + (lo2(v) + hi2(v))) + CC[q, i]

    def cdiverge(s, i):
        v = CU[s, 2, i, CIN]
        return 0.25 * ((CU[s, 0, i, CUP] - CU[s, 0, i, CDN]) + (CU[s, 1, i + 1, CIN] - CU[s, 1, i - 1, CIN])
                       + csgn[i] * (hi2(v) - lo2(v)))

    for q in range(3):
        for copy in ex[q]:
            copy.wait_recv()
        for n, base in ((0, -4), (3, 4), (1, -8), (4, 8)):
            for h in range(2):
                I = C0 + base + 2 * h
                for o, v in zip((I, I + 1), take(n, q, h)):
                    CU[0, q, o, CIN] = v
                    CC[q, o] = v
        CU[0, q, 0, CIN] = take(2, q, 1)[1]
        CU[0, q, 21, CIN] = take(5, q, 0)[0]
        rows(1, 21, lambda i: csweep(0, q, i))
        rows(2, 20, lambda i: csweep(1, q, i))

    for copy in ex[3]:
        copy.wait_recv()
    for n, I, h in ((0, -4, 0), (0, -2, 1), (3, 4, 0), (3, 6, 1), (1, -6, 1), (4, 8, 0)):
        for f, ref in ((3, CE), (4, CG)):
            ref[C0 + I], ref[C0 + I + 1] = take(n, f, h)

    def cpress1(i):
        CP[i, CIN] = -TAU * CE[i] * (cdiverge(0, i) + CG[i])

    rows(3, 19, cpress1)

    def cfirst(i):
        v = CP[i, CIN]
        scale = (-B) / CE[i]
        CC[0, i] = CC[0, i] + scale * (CP[i, CUP] - CP[i, CDN])
        CC[1, i] = CC[1, i] + scale * (CP[i + 1, CIN] - CP[i - 1, CIN])
        CC[2, i] = CC[2, i] + scale * (csgn[i] * (hi2(v) - lo2(v)))
        for q in range(3):
            csweep(0, q, i)

    rows(4, 18, cfirst)
    for q in range(3):
        rows(5, 17, lambda i: csweep(1, q, i))
    for q in range(3):
        rows(6, 16, lambda i: csweep(0, q, i))

    def spread(f, m, v):
        X[f, m, pl.ds(0, 8, stride=2)] = v
        X[f, m, pl.ds(1, 8, stride=2)] = v

    def back_up_p(i):
        spread(3, i - 7, CP[i, CIN] - TAU * CE[i] * (cdiverge(1, i) + CG[i]))

    rows(7, 15, back_up_p)
    turns = (turned(flip_l, back), turned(flip_r, back))
    for copy in halo[3]:
        copy.wait_recv()
    for side, prow in ((0, 4), (1, 17)):
        for n in range(3):
            PB[prow + n, IN] = turns[side](HP_R[side, n])

    def add_p(m):
        for n in range(2):
            PF[4 + 2 * m + n, IN] = PB[4 + 2 * m + n, IN] + X[3, m]

    rows(0, 8, add_p)

    mine = pl.ds(pl.multiple_of(r * 8, 8), 8)

    def place(f):
        return uo_ref.at[f] if f < 3 else po_ref

    def home(f, step):
        rt = jnp.where(r + step >= 4, r + step - 4, r + step)
        return remote(OUT.at[f, pl.ds(4 * rt, 4)], place(f).at[:, mine], os_.at[f, step], or_.at[f], (g, d, rt))

    def own(f):
        return pltpu.make_async_copy(OUT.at[f, layers], place(f).at[:, mine], ol.at[f])

    def send_home(f):
        for step in (2, 1, 3):
            home(f, step).start()
        own(f).start()

    for q in range(3):
        for copy in halo[q]:
            copy.wait_recv()
        for side, urow in ((0, 4), (1, 18)):
            for n in range(2):
                U[1, q, urow + n, IN] = turns[side](HU_R[side, q, n])
        rows(7, 15, lambda i: spread(q, i - 7, CU[1, q, i, CIN]))

        def add_u(m):
            for n in range(2):
                U[0, q, 4 + 2 * m + n, IN] = U[1, q, 4 + 2 * m + n, IN] + X[q, m]

        rows(0, 8, add_u)
        for copy in halo[q]:
            copy.wait_send()
        rows(5, 19, lambda i: push(PF, KB[i], q, i))
        rows(5, 19, lambda i: sweep(0, q, i))
        rows(6, 18, lambda i: sweep(1, q, i))
        rows(7, 17, lambda i: sweep(0, q, i))
        rows(0, 8, lambda a: set_column(OUT.at[q], a, U[1, q, R0 + a, IN]))
        send_home(q)

    def finish_p(a):
        i = R0 + a
        set_column(OUT.at[3], a, PF[i, IN] - TAU * EB[i] * diverge(1, i, 1.0))

    rows(0, 8, finish_p)
    send_home(3)

    def finish_t(a):
        i = R0 + a
        t = TB[i, IN]
        up, dn, nx, pv, hi, lo = TB[i, UP], TB[i, DN], TB[i + 1, IN], TB[i - 1, IN], hi1(t), lo1(t)
        lap = 6.0 * t - (((up + dn) + (nx + pv)) + (hi + lo))
        carried = 0.5 * (U[1, 0, i, IN] * (up - dn) + U[1, 1, i, IN] * (nx - pv) + U[1, 2, i, IN] * (hi - lo))
        set_column(to_ref, a, t + TIME_STEP * (-KAPPA * lap - carried))

    rows(0, 8, finish_t)

    for copy in halo[3]:
        copy.wait_send()
    for copy in heat:
        copy.wait_send()
    for n in range(5):
        for copy in lateral(n):
            copy.wait_send()
    for group in ex:
        for copy in group:
            copy.wait_send()
    for rt in range(4):
        @pl.when(r != rt)
        def _():
            for n in range(5):
                across(n, rt).wait_send()
    for f in range(4):
        for step in (2, 1, 3):
            home(f, step).wait_send()
        own(f).wait()
    for f in range(4):
        landed(place(f).at[:, pl.ds(0, 24)], or_.at[f])


def write_out(*refs):
    sem = refs[6]
    copies = [pltpu.make_async_copy(refs[n], refs[3 + n], sem.at[n]) for n in range(3)]
    for copy in copies:
        copy.start()
    for copy in copies:
        copy.wait()


def per_device(n_dia, n_chain, t, u, p, e, flags):
    f32 = jnp.float32
    V = pltpu.VMEM
    DMA = pltpu.SemaphoreType.DMA
    any_ = pl.BlockSpec(memory_space=pl.ANY)
    vmem = pl.BlockSpec(memory_space=pltpu.VMEM)
    done = pl.pallas_call(
        functools.partial(kernel, n_dia, n_chain, flags.shape[0]),
        out_shape=(
            V(u.shape, f32),
            V(p.shape, f32),
            V(t.shape, f32),
        ),
        in_specs=[any_] * 5,
        out_specs=(vmem,) * 3,
        scratch_shapes=[
            V((3, 16, 24, 128), f32), V((16, 24, 128), f32), V((16, 24, 128), f32), V((16, 24, 128), f32),
            V((2, 3, 24, 32, 128), f32), V((24, 32, 128), f32), V((24, 32, 128), f32),
            V((24, 16, 128), f32), V((24, 16, 128), f32), V((24, 32, 128), f32),
            V((3, 24, 16, 128), f32), V((24, 16, 128), f32), V((5, 4, 16, 128), f32),
            V((5, 2, 8, 128), f32), V((6, 5, 2, 8, 128), f32),
            V((2, 3, 22, 24, 128), f32), V((3, 22, 8, 128), f32), V((22, 8, 128), f32), V((22, 8, 128), f32),
            V((22, 24, 128), f32), V((4, 8, 16, 128), f32),
            V((2, 3, 2, 16, 128), f32), V((2, 3, 16, 128), f32),
            V((4, 16, 8, 128), f32),
            pltpu.SMEM(flags.shape, jnp.int32), pltpu.SMEM((24,), f32), pltpu.SMEM((22,), f32), pltpu.SMEM((6,), jnp.int32),
            DMA((6, 6)), DMA((11,)), DMA((6,)), DMA((8,)), DMA((8,)), DMA((5, 6)), DMA((5, 6)),
            DMA((4, 4)), DMA((4,)), DMA((4,)), DMA, pltpu.SemaphoreType.REGULAR,
        ],
        compiler_params=pltpu.CompilerParams(collective_id=0, has_side_effects=True),
        name="cycle",
    )(t, u, p, e, flags)
    return pl.pallas_call(
        write_out,
        out_shape=[jax.ShapeDtypeStruct(x.shape, f32) for x in done],
        in_specs=[vmem] * 3,
        out_specs=[any_] * 3,
        scratch_shapes=[DMA((3,))],
        name="write_out",
    )(*[pltpu.with_memory_space_constraint(x, pltpu.VMEM) for x in done])


def solution(mesh):
    n_dia = mesh.shape["dia"]
    n_chain = n_dia * mesh.shape["grp"] * mesh.shape["rad"]
    return jax.shard_map(
        functools.partial(per_device, n_dia, n_chain),
        mesh=mesh,
        in_specs=(
            P(None, ("grp", "dia", "rad"), None),
            P(None, "rad", ("grp", "dia"), None),
            P("rad", ("grp", "dia"), None),
            P("rad", ("grp", "dia"), None),
            P(),
        ),
        out_specs=(
            P(None, "rad", ("grp", "dia"), None),
            P("rad", ("grp", "dia"), None),
            P(None, ("grp", "dia", "rad"), None),
        ),
        check_vma=False,
    )
```

```python
import functools

import jax
import jax.numpy as jnp
from jax import lax
from jax.experimental import pallas as pl
from jax.experimental.pallas import tpu as pltpu
from jax.sharding import PartitionSpec as P

DIA_ROWS = 128
OMEGA = 0.8
TAU = 0.25
RAYLEIGH = 4.0
KAPPA = 1.0
TIME_STEP = 0.1
MESH = pl.DeviceIdType.MESH

R0 = 8
HU = 5
HE = 4
IN = pl.ds(8, 16)
UP = pl.ds(9, 16)
DN = pl.ds(7, 16)
CIN = pl.ds(8, 8)
CUP = pl.ds(9, 8)
CDN = pl.ds(7, 8)
C0 = 9
A = 1.0 - OMEGA
B = OMEGA / 6.0


def rows(lo, hi, body, unroll=None):
    unroll = hi - lo if unroll is None else unroll
    lax.fori_loop(lo, hi, lambda i, c: (body(i), c)[1], 0, unroll=unroll)


def column(ref, i):
    layers, width, lanes = ref.shape
    return ref.reshape(layers * width, lanes)[pl.ds(i, layers, stride=width)]


def set_column(ref, i, v):
    layers, width, lanes = ref.shape
    ref.reshape(layers * width, lanes)[pl.ds(i, layers, stride=width)] = v


def span(rt, halo):
    lo, hi = max(0, 8 * rt - halo), min(32, 8 * rt + 8 + halo)
    return lo, hi - lo, lo - 8 * rt + R0


def kernel(
    n_dia, n_chain, n_diamonds,
    t_ref, u_ref, p_ref, e_ref, flag_hbm,
    uo_ref, po_ref, to_ref,
    rawu, rawp, rawe, rawt,
    U, PB, PF, EB, KB, TB, CB, DB, TMP,
    CS, CR, CU, CC, CE, CG, CP, X, HU_R, HP_R, OUT,
    flag_ref, sgn, csgn, cflip,
    gs, gr, ls, hs, hr, xs, xr, os_, or_, ol, fs,
):
    g = lax.axis_index("grp")
    d = lax.axis_index("dia")
    r = lax.axis_index("rad")
    k = g * n_dia + d
    c = k * 4 + r
    n_k = n_chain // 4

    def dev(ci):
        kk = lax.div(ci, 4)
        return (lax.div(kk, n_dia), lax.rem(kk, n_dia), lax.rem(ci, 4))

    def chain(step):
        return dev(lax.rem(c + step + n_chain, n_chain))

    barrier = pltpu.get_barrier_semaphore()
    for step in (1, -1, 2, -2, 3, -3, 4, -4):
        pl.semaphore_signal(barrier, inc=1, device_id=chain(step), device_id_type=MESH)

    pl.semaphore_wait(barrier, 8)

    layers = pl.ds(r * 4, 4)
    srcs = ((p_ref, rawp, HU), (e_ref, rawe, HE)) + tuple((u_ref.at[q], rawu.at[q], HU) for q in range(3))

    def cut(ref, lay, start, size):
        return ref.at[lay, pl.ds(start, size)]

    def remote(src, dst, ssem, rsem, to):
        return pltpu.make_async_remote_copy(
            src_ref=src, dst_ref=dst, send_sem=ssem, recv_sem=rsem, device_id=to, device_id_type=MESH)

    nxt = lax.rem(k + 1, n_k)
    prv = lax.rem(k - 1 + n_k, n_k)
    to_next = (lax.div(nxt, n_dia), lax.rem(nxt, n_dia), 0)
    to_prev = (lax.div(prv, n_dia), lax.rem(prv, n_dia), 3)

    def lateral(n):
        src, dst, halo = srcs[n]
        return [
            remote(cut(src, slice(None), 32 - halo, halo), cut(dst, layers, R0 - halo, halo),
                   gs.at[n, 4], gr.at[5 + n], to_next),
            remote(cut(src, slice(None), 0, halo), cut(dst, layers, R0 + 8, halo),
                   gs.at[n, 5], gr.at[5 + n], to_prev)]

    def across(n, rt):
        src, dst, halo = srcs[n]
        lo, size, at = span(rt, halo)
        return remote(cut(src, slice(None), lo, size), cut(dst, layers, at, size), gs.at[n, rt], gr.at[n], (g, d, rt))

    heat = [
        remote(t_ref.at[:, pl.ds(8 - HE, HE)], rawt.at[:, pl.ds(R0 - HE, HE)], gs.at[5, 0], gr.at[10], chain(1)),
        remote(t_ref.at[:, pl.ds(0, HE)], rawt.at[:, pl.ds(R0 + 8, HE)], gs.at[5, 1], gr.at[10], chain(-1))]
    for rs in range(4):
        @pl.when(r == rs)
        def _():
            for copy in heat:
                copy.start()
            for n in range(5):
                for copy in lateral(n):
                    copy.start()
            for n in range(5):
                for step in (2, 1, 3):
                    across(n, (rs + step) % 4).start()

    read_flags = pltpu.make_async_copy(flag_hbm, flag_ref, fs)
    read_flags.start()
    for rt in range(4):
        @pl.when(r == rt)
        def _():
            for n, (src, dst, halo) in enumerate(srcs):
                lo, size, at = span(rt, halo)
                pltpu.make_async_copy(cut(src, slice(None), lo, size), cut(dst, layers, at, size), ls.at[n]).start()
    pltpu.make_async_copy(t_ref, rawt.at[:, pl.ds(R0, 8)], ls.at[5]).start()

    z = jnp.zeros((8, 128), jnp.float32)

    def clear(i):
        for s in range(2):
            for q in range(3):
                U[s, q, i, pl.ds(0, 8)] = z
                U[s, q, i, pl.ds(24, 8)] = z
        for ref in (PB, PF, TB):
            ref[i, pl.ds(0, 8)] = z
            ref[i, pl.ds(24, 8)] = z

    rows(0, 24, clear, 1)

    def cclear(i):
        for s in range(2):
            for q in range(3):
                CU[s, q, i, pl.ds(0, 8)] = z
                CU[s, q, i, pl.ds(16, 8)] = z
        CP[i, pl.ds(0, 8)] = z
        CP[i, pl.ds(16, 8)] = z

    rows(0, 22, cclear, 1)

    read_flags.wait()
    per = DIA_ROWS // 32
    left = jnp.where((lax.rem(k, per) == 0) & (flag_ref[lax.div(k, per)] == 1), 1, 0)
    right = jnp.where(
        (lax.rem(k + 1, per) == 0) & (flag_ref[lax.rem(lax.div(k + 1, per), n_diamonds)] == 1), 1, 0)

    def flip_of(j, width, block):
        return jnp.where(j < -width * r, left, jnp.where(j >= block - width * r, right, 0))

    for i in range(24):
        sgn[i] = jnp.where(flip_of(i - R0, 8, 32) == 1, -1.0, 1.0)
    for i in range(22):
        csgn[i] = jnp.where(flip_of(i - C0, 4, 16) == 1, -1.0, 1.0)
    for n, J in enumerate((-4, -8, -12, 4, 8, 12)):
        cflip[n] = flip_of(J, 4, 16)
    flip_l, flip_r = flip_of(-1, 8, 32), flip_of(8, 8, 32)

    lane = lax.broadcasted_iota(jnp.int32, (16, 128), 1)
    clane = lax.broadcasted_iota(jnp.int32, (8, 128), 1)
    even = lax.rem(clane, 2) == 0
    back = 127 - lane
    cback = 127 - clane

    def lo1(v):
        return jnp.where(lane == 0, 0.0, pltpu.roll(v, 1, 1))

    def hi1(v):
        return jnp.where(lane == 127, 0.0, pltpu.roll(v, 127, 1))

    def lo2(v):
        return jnp.where(clane < 2, 0.0, pltpu.roll(v, 2, 1))

    def hi2(v):
        return jnp.where(clane >= 126, 0.0, pltpu.roll(v, 126, 1))

    def landed(ref, sem):
        pltpu.make_async_copy(ref, ref, sem).wait()

    def gathered(which):
        for rt in range(4):
            @pl.when(r == rt)
            def _():
                for n in which:
                    src, dst, halo = srcs[n]
                    lo, size, at = span(rt, halo)
                    landed(cut(dst, slice(0, 4), at, size), ls.at[n])
                    landed(cut(dst, slice(0, 12), at, size), gr.at[n])
                    if rt in (0, 3):
                        landed(cut(dst, slice(0, 16), at, halo), gr.at[5 + n])

    gathered((0, 1))
    landed(rawt.at[:, pl.ds(R0, 8)], ls.at[5])
    landed(rawt.at[:, pl.ds(R0, 2 * HE)], gr.at[10])

    def put_scalars(i, turn):
        PB[i, IN] = turn(column(rawp, i))
        EB[i] = turn(column(rawe, i))
        TB[i, IN] = turn(column(rawt, i))

    def put_vector(q, i, turn):
        U[0, q, i, IN] = turn(column(rawu.at[q], i))

    def turned(flag, idx):
        return lambda v: jnp.where(flag == 1, jnp.take_along_axis(v, idx, axis=1), v)

    def put_all(put):
        rows(8, 16, lambda i: put(i, lambda v: v))
        rows(R0 - HU, R0, lambda i: put(i, turned(flip_l, back)))
        rows(R0 + 8, R0 + 8 + HU, lambda i: put(i, turned(flip_r, back)))

    put_all(put_scalars)

    def stencil(ref, s, q, i):
        v = ref[s, q, i, IN]
        total = (ref[s, q, i, UP] + ref[s, q, i, DN]) + (ref[s, q, i + 1, IN] + ref[s, q, i - 1, IN])
        return v, total + (lo1(v) + hi1(v))

    def sweep(s, q, i):
        v, total = stencil(U, s, q, i)
        U[1 - s, q, i, IN] = A * v + B * total + CB[q, i]

    def slope(ref, i, sign):
        v = ref[i, IN]
        return (ref[i, UP] - ref[i, DN], ref[i + 1, IN] - ref[i - 1, IN], sign * (hi1(v) - lo1(v)))

    def diverge(s, i, sign):
        v = U[s, 2, i, IN]
        return 0.5 * ((U[s, 0, i, UP] - U[s, 0, i, DN]) + (U[s, 1, i + 1, IN] - U[s, 1, i - 1, IN])
                      + sign * (hi1(v) - lo1(v)))

    def push(press, kinv, i):
        gr_, ga_, gb_ = slope(press, i, sgn[i])
        half = -0.5 * kinv
        CB[0, i] = kinv * (RAYLEIGH * TB[i, IN]) + half * gr_
        CB[1, i] = half * ga_
        CB[2, i] = half * gb_

    def first_push(i):
        kinv = B / EB[i]
        KB[i] = kinv
        push(PB, kinv, i)

    rows(4, 20, first_push)
    for q in range(3):
        gathered((2 + q,))
        put_all(functools.partial(put_vector, q))
        rows(4, 20, lambda i: sweep(0, q, i))
        rows(5, 19, lambda i: sweep(1, q, i))
        rows(6, 18, lambda i: sweep(0, q, i))

    halo = []
    for q in range(3):
        halo.append((remote(U.at[1, q, pl.ds(R0 + 4, 2), IN], HU_R.at[0, q], hs.at[2 * q], hr.at[2 * q], chain(1)),
                     remote(U.at[1, q, pl.ds(R0 + 2, 2), IN], HU_R.at[1, q], hs.at[2 * q + 1], hr.at[2 * q + 1], chain(-1))))
    halo.append((remote(PB.at[pl.ds(R0 + 4, 3), IN], HP_R.at[0], hs.at[6], hr.at[6], chain(1)),
                 remote(PB.at[pl.ds(R0 + 1, 3), IN], HP_R.at[1], hs.at[7], hr.at[7], chain(-1))))

    def pre_pressure(i):
        div = diverge(1, i, sgn[i])
        DB[i] = div
        PB[i, IN] = PB[i, IN] - TAU * EB[i] * div

    rows(7, 17, pre_pressure)

    def restrict(f, m, acc):
        TMP[f, m] = acc
        v = TMP[f, m, pl.ds(0, 8, stride=2)] + TMP[f, m, pl.ds(1, 8, stride=2)]
        return 0.125 * (v + jnp.where(even, pltpu.roll(v, 127, 1), pltpu.roll(v, 1, 1)))

    def pack(f, vals):
        for h in range(2):
            CS[f, h] = jnp.where(even, vals[2 * h], vals[2 * h + 1])

    def residual(q, ii):
        v, total = stencil(U, 1, q, ii)
        w = PB[ii, IN]
        if q == 0:
            gp = PB[ii, UP] - PB[ii, DN]
        elif q == 1:
            gp = PB[ii + 1, IN] - PB[ii - 1, IN]
        else:
            gp = hi1(w) - lo1(w)
        res = -0.5 * gp - EB[ii] * (6.0 * v - total)
        return res + RAYLEIGH * TB[ii, IN] if q == 0 else res

    def send_vector(q):
        one = pl.ds(q, 1)
        out = [
            remote(CS.at[one], CR.at[1, one], xs.at[q, 1], xr.at[q, 1], chain(2)),
            remote(CS.at[one], CR.at[4, one], xs.at[q, 4], xr.at[q, 4], chain(-2)),
            remote(CS.at[one, pl.ds(1, 1)], CR.at[2, one, pl.ds(1, 1)], xs.at[q, 2], xr.at[q, 2], chain(3)),
            remote(CS.at[one, pl.ds(0, 1)], CR.at[5, one, pl.ds(0, 1)], xs.at[q, 5], xr.at[q, 5], chain(-3)),
            remote(CS.at[one], CR.at[0, one], xs.at[q, 0], xr.at[q, 0], chain(1)),
            remote(CS.at[one], CR.at[3, one], xs.at[q, 3], xr.at[q, 3], chain(-1)),
        ]
        for copy in out:
            copy.start()
        return out

    ce = [restrict(3, m, EB[R0 + 2 * m] + EB[R0 + 2 * m + 1]) for m in range(4)]
    cg = [restrict(4, m, DB[R0 + 2 * m] + DB[R0 + 2 * m + 1]) for m in range(4)]
    cinv = [(4.0 * B) / e for e in ce]
    ex = []
    for q in range(3):
        vals = [cinv[m] * restrict(q, m, residual(q, R0 + 2 * m) + residual(q, R0 + 2 * m + 1)) for m in range(4)]
        pack(q, vals)
        ex.append(send_vector(q))
        for m in range(4):
            CU[0, q, C0 + m, CIN] = vals[m]
            CC[q, C0 + m] = vals[m]
    pack(3, ce)
    pack(4, cg)
    both = pl.ds(3, 2)
    ex.append([
        remote(CS.at[both, pl.ds(1, 1)], CR.at[1, both, pl.ds(1, 1)], xs.at[3, 1], xr.at[3, 1], chain(2)),
        remote(CS.at[both, pl.ds(0, 1)], CR.at[4, both, pl.ds(0, 1)], xs.at[3, 4], xr.at[3, 4], chain(-2)),
        remote(CS.at[both], CR.at[0, both], xs.at[3, 0], xr.at[3, 0], chain(1)),
        remote(CS.at[both], CR.at[3, both], xs.at[3, 3], xr.at[3, 3], chain(-1)),
    ])
    for copy in ex[3]:
        copy.start()
    for pair in (halo[3],) + tuple(halo[:3]):
        for copy in pair:
            copy.start()
    for m in range(4):
        CE[C0 + m] = ce[m]
        CG[C0 + m] = cg[m]

    def unpack(x):
        return (jnp.where(even, x, pltpu.roll(x, 1, 1)), jnp.where(even, pltpu.roll(x, 127, 1), x))

    def take(n, f, h):
        turn = turned(cflip[n], cback)
        a, b = unpack(CR[n, f, h])
        return turn(a), turn(b)

    def csweep(s, q, i):
        v = CU[s, q, i, CIN]
        total = (CU[s, q, i, CUP] + CU[s, q, i, CDN]) + (CU[s, q, i + 1, CIN] + CU[s, q, i - 1, CIN])
        CU[1 - s, q, i, CIN] = A * v + B * (total + (lo2(v) + hi2(v))) + CC[q, i]

    def cdiverge(s, i):
        v = CU[s, 2, i, CIN]
        return 0.25 * ((CU[s, 0, i, CUP] - CU[s, 0, i, CDN]) + (CU[s, 1, i + 1, CIN] - CU[s, 1, i - 1, CIN])
                       + csgn[i] * (hi2(v) - lo2(v)))

    for q in range(3):
        for copy in ex[q]:
            copy.wait_recv()
        for n, base in ((0, -4), (3, 4), (1, -8), (4, 8)):
            for h in range(2):
                I = C0 + base + 2 * h
                for o, v in zip((I, I + 1), take(n, q, h)):
                    CU[0, q, o, CIN] = v
                    CC[q, o] = v
        CU[0, q, 0, CIN] = take(2, q, 1)[1]
        CU[0, q, 21, CIN] = take(5, q, 0)[0]
        rows(1, 21, lambda i: csweep(0, q, i))
        rows(2, 20, lambda i: csweep(1, q, i))

    for copy in ex[3]:
        copy.wait_recv()
    for n, I, h in ((0, -4, 0), (0, -2, 1), (3, 4, 0), (3, 6, 1), (1, -6, 1), (4, 8, 0)):
        for f, ref in ((3, CE), (4, CG)):
            ref[C0 + I], ref[C0 + I + 1] = take(n, f, h)

    def cpress1(i):
        CP[i, CIN] = -TAU * CE[i] * (cdiverge(0, i) + CG[i])

    rows(3, 19, cpress1)

    def cfirst(i):
        v = CP[i, CIN]
        scale = (-B) / CE[i]
        CC[0, i] = CC[0, i] + scale * (CP[i, CUP] - CP[i, CDN])
        CC[1, i] = CC[1, i] + scale * (CP[i + 1, CIN] - CP[i - 1, CIN])
        CC[2, i] = CC[2, i] + scale * (csgn[i] * (hi2(v) - lo2(v)))
        for q in range(3):
            csweep(0, q, i)

    rows(4, 18, cfirst)
    for q in range(3):
        rows(5, 17, lambda i: csweep(1, q, i))
    for q in range(3):
        rows(6, 16, lambda i: csweep(0, q, i))

    def spread(f, m, v):
        X[f, m, pl.ds(0, 8, stride=2)] = v
        X[f, m, pl.ds(1, 8, stride=2)] = v

    def back_up_p(i):
        spread(3, i - 7, CP[i, CIN] - TAU * CE[i] * (cdiverge(1, i) + CG[i]))

    rows(7, 15, back_up_p)
    turns = (turned(flip_l, back), turned(flip_r, back))
    for copy in halo[3]:
        copy.wait_recv()
    for side, prow in ((0, 4), (1, 17)):
        for n in range(3):
            PB[prow + n, IN] = turns[side](HP_R[side, n])

    def add_p(m):
        for n in range(2):
            PF[4 + 2 * m + n, IN] = PB[4 + 2 * m + n, IN] + X[3, m]

    rows(0, 8, add_p)
    rows(5, 19, lambda i: push(PF, KB[i], i))

    mine = pl.ds(pl.multiple_of(r * 8, 8), 8)

    def place(f):
        return uo_ref.at[f] if f < 3 else po_ref

    def home(f, step):
        rt = lax.rem(r + step, 4)
        return remote(OUT.at[f, pl.ds(4 * rt, 4)], place(f).at[:, mine], os_.at[f, step], or_.at[f], (g, d, rt))

    def own(f):
        return pltpu.make_async_copy(OUT.at[f, layers], place(f).at[:, mine], ol.at[f])

    def send_home(f):
        for step in (2, 1, 3):
            home(f, step).start()
        own(f).start()

    for q in range(3):
        for copy in halo[q]:
            copy.wait_recv()
        for side, urow in ((0, 4), (1, 18)):
            for n in range(2):
                U[1, q, urow + n, IN] = turns[side](HU_R[side, q, n])
        rows(7, 15, lambda i: spread(q, i - 7, CU[1, q, i, CIN]))

        def add_u(m):
            for n in range(2):
                U[0, q, 4 + 2 * m + n, IN] = U[1, q, 4 + 2 * m + n, IN] + X[q, m]

        rows(0, 8, add_u)
        for copy in halo[q]:
            copy.wait_send()
        rows(5, 19, lambda i: sweep(0, q, i))
        rows(6, 18, lambda i: sweep(1, q, i))
        rows(7, 17, lambda i: sweep(0, q, i))
        rows(0, 8, lambda a: set_column(OUT.at[q], a, U[1, q, R0 + a, IN]))
        send_home(q)

    def finish_p(a):
        i = R0 + a
        set_column(OUT.at[3], a, PF[i, IN] - TAU * EB[i] * diverge(1, i, 1.0))

    rows(0, 8, finish_p)
    send_home(3)

    def finish_t(a):
        i = R0 + a
        t = TB[i, IN]
        up, dn, nx, pv, hi, lo = TB[i, UP], TB[i, DN], TB[i + 1, IN], TB[i - 1, IN], hi1(t), lo1(t)
        lap = 6.0 * t - (((up + dn) + (nx + pv)) + (hi + lo))
        carried = 0.5 * (U[1, 0, i, IN] * (up - dn) + U[1, 1, i, IN] * (nx - pv) + U[1, 2, i, IN] * (hi - lo))
        set_column(to_ref, a, t + TIME_STEP * (-KAPPA * lap - carried))

    rows(0, 8, finish_t)

    for copy in halo[3]:
        copy.wait_send()
    for copy in heat:
        copy.wait_send()
    for n in range(5):
        for copy in lateral(n):
            copy.wait_send()
    for group in ex:
        for copy in group:
            copy.wait_send()
    for rt in range(4):
        @pl.when(r != rt)
        def _():
            for n in range(5):
                across(n, rt).wait_send()
    for f in range(4):
        for step in (2, 1, 3):
            home(f, step).wait_send()
        own(f).wait()
    for f in range(4):
        landed(place(f).at[:, pl.ds(0, 24)], or_.at[f])


def write_out(*refs):
    sem = refs[6]
    copies = [pltpu.make_async_copy(refs[n], refs[3 + n], sem.at[n]) for n in range(3)]
    for copy in copies:
        copy.start()
    for copy in copies:
        copy.wait()


def per_device(n_dia, n_chain, t, u, p, e, flags):
    f32 = jnp.float32
    V = pltpu.VMEM
    DMA = pltpu.SemaphoreType.DMA
    any_ = pl.BlockSpec(memory_space=pl.ANY)
    vmem = pl.BlockSpec(memory_space=pltpu.VMEM)
    done = pl.pallas_call(
        functools.partial(kernel, n_dia, n_chain, flags.shape[0]),
        out_shape=(
            V(u.shape, f32),
            V(p.shape, f32),
            V(t.shape, f32),
        ),
        in_specs=[any_] * 5,
        out_specs=(vmem,) * 3,
        scratch_shapes=[
            V((3, 16, 24, 128), f32), V((16, 24, 128), f32), V((16, 24, 128), f32), V((16, 24, 128), f32),
            V((2, 3, 24, 32, 128), f32), V((24, 32, 128), f32), V((24, 32, 128), f32),
            V((24, 16, 128), f32), V((24, 16, 128), f32), V((24, 32, 128), f32),
            V((3, 24, 16, 128), f32), V((24, 16, 128), f32), V((5, 4, 16, 128), f32),
            V((5, 2, 8, 128), f32), V((6, 5, 2, 8, 128), f32),
            V((2, 3, 22, 24, 128), f32), V((3, 22, 8, 128), f32), V((22, 8, 128), f32), V((22, 8, 128), f32),
            V((22, 24, 128), f32), V((4, 8, 16, 128), f32),
            V((2, 3, 2, 16, 128), f32), V((2, 3, 16, 128), f32),
            V((4, 16, 8, 128), f32),
            pltpu.SMEM(flags.shape, jnp.int32), pltpu.SMEM((24,), f32), pltpu.SMEM((22,), f32), pltpu.SMEM((6,), jnp.int32),
            DMA((6, 6)), DMA((11,)), DMA((6,)), DMA((8,)), DMA((8,)), DMA((4, 6)), DMA((4, 6)),
            DMA((4, 4)), DMA((4,)), DMA((4,)), DMA,
        ],
        compiler_params=pltpu.CompilerParams(collective_id=0, has_side_effects=True),
        name="cycle",
    )(t, u, p, e, flags)
    return pl.pallas_call(
        write_out,
        out_shape=[jax.ShapeDtypeStruct(x.shape, f32) for x in done],
        in_specs=[vmem] * 3,
        out_specs=[any_] * 3,
        scratch_shapes=[DMA((3,))],
        name="write_out",
    )(*[pltpu.with_memory_space_constraint(x, pltpu.VMEM) for x in done])


def solution(mesh):
    n_dia = mesh.shape["dia"]
    n_chain = n_dia * mesh.shape["grp"] * mesh.shape["rad"]
    return jax.shard_map(
        functools.partial(per_device, n_dia, n_chain),
        mesh=mesh,
        in_specs=(
            P(None, ("grp", "dia", "rad"), None),
            P(None, "rad", ("grp", "dia"), None),
            P("rad", ("grp", "dia"), None),
            P("rad", ("grp", "dia"), None),
            P(),
        ),
        out_specs=(
            P(None, "rad", ("grp", "dia"), None),
            P("rad", ("grp", "dia"), None),
            P(None, ("grp", "dia", "rad"), None),
        ),
        check_vma=False,
    )
```

```python
import functools

import jax
import jax.numpy as jnp
from jax import lax
from jax.experimental import pallas as pl
from jax.experimental.pallas import tpu as pltpu
from jax.sharding import PartitionSpec as P

DIA_ROWS = 128
OMEGA = 0.8
TAU = 0.25
RAYLEIGH = 4.0
KAPPA = 1.0
TIME_STEP = 0.1
MESH = pl.DeviceIdType.MESH

R0 = 8
HU = 5
HE = 4
IN = pl.ds(8, 16)
UP = pl.ds(9, 16)
DN = pl.ds(7, 16)
CIN = pl.ds(8, 8)
CUP = pl.ds(9, 8)
CDN = pl.ds(7, 8)
C0 = 9
A = 1.0 - OMEGA
B = OMEGA / 6.0


def rows(lo, hi, body, unroll=None):
    unroll = hi - lo if unroll is None else unroll
    lax.fori_loop(lo, hi, lambda i, c: (body(i), c)[1], 0, unroll=unroll)


def column(ref, i):
    layers, width, lanes = ref.shape
    return ref.reshape(layers * width, lanes)[pl.ds(i, layers, stride=width)]


def set_column(ref, i, v):
    layers, width, lanes = ref.shape
    ref.reshape(layers * width, lanes)[pl.ds(i, layers, stride=width)] = v


def span(rt, halo):
    lo, hi = max(0, 8 * rt - halo), min(32, 8 * rt + 8 + halo)
    return lo, hi - lo, lo - 8 * rt + R0


def kernel(
    n_dia, n_chain, n_diamonds,
    t_ref, u_ref, p_ref, e_ref, flag_hbm,
    uo_ref, po_ref, to_ref,
    rawu, rawp, rawe, rawt,
    U, PB, PF, EB, KB, TB, CB, DB, TMP,
    CS, CR, CU, CC, CE, CG, CP, X, HU_R, HP_R, OUT,
    flag_ref, sgn, csgn, cflip,
    gs, gr, ls, hs, hr, xs, xr, os_, or_, ol, fs,
):
    g = lax.axis_index("grp")
    d = lax.axis_index("dia")
    r = lax.axis_index("rad")
    k = g * n_dia + d
    n_k = n_chain // 4
    n_grp = n_k // n_dia

    over = d == n_dia - 1
    under = d == 0
    next_g = jnp.where(over, jnp.where(g == n_grp - 1, 0, g + 1), g)
    next_d = jnp.where(over, 0, d + 1)
    prev_g = jnp.where(under, jnp.where(g == 0, n_grp - 1, g - 1), g)
    prev_d = jnp.where(under, n_dia - 1, d - 1)
    to_next, to_prev = (next_g, next_d, 0), (prev_g, prev_d, 3)
    chains = {4: (next_g, next_d, r), -4: (prev_g, prev_d, r)}
    for step in (1, 2, 3):
        out = r + step >= 4
        chains[step] = (jnp.where(out, next_g, g), jnp.where(out, next_d, d), jnp.where(out, r + step - 4, r + step))
        out = r - step < 0
        chains[-step] = (jnp.where(out, prev_g, g), jnp.where(out, prev_d, d), jnp.where(out, r - step + 4, r - step))

    def chain(step):
        return chains[step]

    barrier = pltpu.get_barrier_semaphore()
    for step in (1, -1, 2, -2, 3, -3, 4, -4):
        pl.semaphore_signal(barrier, inc=1, device_id=chain(step), device_id_type=MESH)

    pl.semaphore_wait(barrier, 8)

    layers = pl.ds(r * 4, 4)
    srcs = ((p_ref, rawp, HU), (e_ref, rawe, HE)) + tuple((u_ref.at[q], rawu.at[q], HU) for q in range(3))

    def cut(ref, lay, start, size):
        return ref.at[lay, pl.ds(start, size)]

    def remote(src, dst, ssem, rsem, to):
        return pltpu.make_async_remote_copy(
            src_ref=src, dst_ref=dst, send_sem=ssem, recv_sem=rsem, device_id=to, device_id_type=MESH)

    def lateral(n):
        src, dst, halo = srcs[n]
        return [
            remote(cut(src, slice(None), 32 - halo, halo), cut(dst, layers, R0 - halo, halo),
                   gs.at[n, 4], gr.at[5 + n], to_next),
            remote(cut(src, slice(None), 0, halo), cut(dst, layers, R0 + 8, halo),
                   gs.at[n, 5], gr.at[5 + n], to_prev)]

    def across(n, rt):
        src, dst, halo = srcs[n]
        lo, size, at = span(rt, halo)
        return remote(cut(src, slice(None), lo, size), cut(dst, layers, at, size), gs.at[n, rt], gr.at[n], (g, d, rt))

    heat = [
        remote(t_ref.at[:, pl.ds(8 - HE, HE)], rawt.at[:, pl.ds(R0 - HE, HE)], gs.at[5, 0], gr.at[10], chain(1)),
        remote(t_ref.at[:, pl.ds(0, HE)], rawt.at[:, pl.ds(R0 + 8, HE)], gs.at[5, 1], gr.at[10], chain(-1))]
    for rs in range(4):
        @pl.when(r == rs)
        def _():
            for copy in heat:
                copy.start()
            for n in range(5):
                for copy in lateral(n):
                    copy.start()
            for n in range(5):
                for step in (2, 1, 3):
                    across(n, (rs + step) % 4).start()

    read_flags = pltpu.make_async_copy(flag_hbm, flag_ref, fs)
    read_flags.start()
    for rt in range(4):
        @pl.when(r == rt)
        def _():
            for n, (src, dst, halo) in enumerate(srcs):
                lo, size, at = span(rt, halo)
                pltpu.make_async_copy(cut(src, slice(None), lo, size), cut(dst, layers, at, size), ls.at[n]).start()
    pltpu.make_async_copy(t_ref, rawt.at[:, pl.ds(R0, 8)], ls.at[5]).start()

    z = jnp.zeros((8, 128), jnp.float32)

    def clear(i):
        for s in range(2):
            for q in range(3):
                U[s, q, i, pl.ds(0, 8)] = z
                U[s, q, i, pl.ds(24, 8)] = z
        for ref in (PB, PF, TB):
            ref[i, pl.ds(0, 8)] = z
            ref[i, pl.ds(24, 8)] = z

    rows(0, 24, clear, 1)

    def cclear(i):
        for s in range(2):
            for q in range(3):
                CU[s, q, i, pl.ds(0, 8)] = z
                CU[s, q, i, pl.ds(16, 8)] = z
        CP[i, pl.ds(0, 8)] = z
        CP[i, pl.ds(16, 8)] = z

    rows(0, 22, cclear, 1)

    read_flags.wait()
    per = DIA_ROWS // 32
    left = jnp.where((lax.rem(k, per) == 0) & (flag_ref[lax.div(k, per)] == 1), 1, 0)
    right = jnp.where(
        (lax.rem(k + 1, per) == 0) & (flag_ref[lax.rem(lax.div(k + 1, per), n_diamonds)] == 1), 1, 0)

    def flip_of(j, width, block):
        return jnp.where(j < -width * r, left, jnp.where(j >= block - width * r, right, 0))

    for i in range(24):
        sgn[i] = jnp.where(flip_of(i - R0, 8, 32) == 1, -1.0, 1.0)
    for i in range(22):
        csgn[i] = jnp.where(flip_of(i - C0, 4, 16) == 1, -1.0, 1.0)
    for n, J in enumerate((-4, -8, -12, 4, 8, 12)):
        cflip[n] = flip_of(J, 4, 16)
    flip_l, flip_r = flip_of(-1, 8, 32), flip_of(8, 8, 32)

    lane = lax.broadcasted_iota(jnp.int32, (16, 128), 1)
    clane = lax.broadcasted_iota(jnp.int32, (8, 128), 1)
    even = lax.rem(clane, 2) == 0
    back = 127 - lane
    cback = 127 - clane

    def lo1(v):
        return jnp.where(lane == 0, 0.0, pltpu.roll(v, 1, 1))

    def hi1(v):
        return jnp.where(lane == 127, 0.0, pltpu.roll(v, 127, 1))

    def lo2(v):
        return jnp.where(clane < 2, 0.0, pltpu.roll(v, 2, 1))

    def hi2(v):
        return jnp.where(clane >= 126, 0.0, pltpu.roll(v, 126, 1))

    def landed(ref, sem):
        pltpu.make_async_copy(ref, ref, sem).wait()

    def gathered(which):
        for rt in range(4):
            @pl.when(r == rt)
            def _():
                for n in which:
                    src, dst, halo = srcs[n]
                    lo, size, at = span(rt, halo)
                    landed(cut(dst, slice(0, 4), at, size), ls.at[n])
                    landed(cut(dst, slice(0, 12), at, size), gr.at[n])
                    if rt in (0, 3):
                        landed(cut(dst, slice(0, 16), at, halo), gr.at[5 + n])

    gathered((0, 1))
    landed(rawt.at[:, pl.ds(R0, 8)], ls.at[5])
    landed(rawt.at[:, pl.ds(R0, 2 * HE)], gr.at[10])

    def put_scalars(i, turn):
        PB[i, IN] = turn(column(rawp, i))
        EB[i] = turn(column(rawe, i))
        TB[i, IN] = turn(column(rawt, i))

    def put_vector(q, i, turn):
        U[0, q, i, IN] = turn(column(rawu.at[q], i))

    def turned(flag, idx):
        return lambda v: jnp.where(flag == 1, jnp.take_along_axis(v, idx, axis=1), v)

    def put_all(put):
        rows(8, 16, lambda i: put(i, lambda v: v))
        rows(R0 - HU, R0, lambda i: put(i, turned(flip_l, back)))
        rows(R0 + 8, R0 + 8 + HU, lambda i: put(i, turned(flip_r, back)))

    put_all(put_scalars)

    def stencil(ref, s, q, i):
        v = ref[s, q, i, IN]
        total = (ref[s, q, i, UP] + ref[s, q, i, DN]) + (ref[s, q, i + 1, IN] + ref[s, q, i - 1, IN])
        return v, total + (lo1(v) + hi1(v))

    def sweep(s, q, i):
        v, total = stencil(U, s, q, i)
        U[1 - s, q, i, IN] = A * v + B * total + CB[q, i]

    def diverge(s, i, sign):
        v = U[s, 2, i, IN]
        return 0.5 * ((U[s, 0, i, UP] - U[s, 0, i, DN]) + (U[s, 1, i + 1, IN] - U[s, 1, i - 1, IN])
                      + sign * (hi1(v) - lo1(v)))

    def push(press, kinv, q, i):
        half = -0.5 * kinv
        if q == 0:
            CB[0, i] = kinv * (RAYLEIGH * TB[i, IN]) + half * (press[i, UP] - press[i, DN])
        elif q == 1:
            CB[1, i] = half * (press[i + 1, IN] - press[i - 1, IN])
        else:
            v = press[i, IN]
            CB[2, i] = half * (sgn[i] * (hi1(v) - lo1(v)))

    def first_push(i):
        kinv = B / EB[i]
        KB[i] = kinv
        for q in range(3):
            push(PB, kinv, q, i)

    rows(4, 20, first_push)
    def restrict(f, m, acc):
        TMP[f, m] = acc
        v = TMP[f, m, pl.ds(0, 8, stride=2)] + TMP[f, m, pl.ds(1, 8, stride=2)]
        return 0.125 * (v + jnp.where(even, pltpu.roll(v, 127, 1), pltpu.roll(v, 1, 1)))

    def pack(f, vals):
        for h in range(2):
            CS[f, h] = jnp.where(even, vals[2 * h], vals[2 * h + 1])

    def send_scalar(f):
        one = pl.ds(f, 1)
        out = [
            remote(CS.at[one, pl.ds(1, 1)], CR.at[1, one, pl.ds(1, 1)], xs.at[f, 1], xr.at[f, 1], chain(2)),
            remote(CS.at[one, pl.ds(0, 1)], CR.at[4, one, pl.ds(0, 1)], xs.at[f, 4], xr.at[f, 4], chain(-2)),
            remote(CS.at[one], CR.at[0, one], xs.at[f, 0], xr.at[f, 0], chain(1)),
            remote(CS.at[one], CR.at[3, one], xs.at[f, 3], xr.at[f, 3], chain(-1)),
        ]
        for copy in out:
            copy.start()
        return out

    ce = [restrict(3, m, EB[R0 + 2 * m] + EB[R0 + 2 * m + 1]) for m in range(4)]
    cinv = [(4.0 * B) / e for e in ce]
    pack(3, ce)
    for m in range(4):
        CE[C0 + m] = ce[m]

    for q in range(3):
        gathered((2 + q,))
        if q == 2:
            ex_e = send_scalar(3)
        put_all(functools.partial(put_vector, q))
        rows(4, 20, lambda i: sweep(0, q, i))
        rows(5, 19, lambda i: sweep(1, q, i))
        rows(6, 18, lambda i: sweep(0, q, i))

    halo = []
    for q in range(3):
        halo.append((remote(U.at[1, q, pl.ds(R0 + 4, 2), IN], HU_R.at[0, q], hs.at[2 * q], hr.at[2 * q], chain(1)),
                     remote(U.at[1, q, pl.ds(R0 + 2, 2), IN], HU_R.at[1, q], hs.at[2 * q + 1], hr.at[2 * q + 1], chain(-1))))
    halo.append((remote(PB.at[pl.ds(R0 + 4, 3), IN], HP_R.at[0], hs.at[6], hr.at[6], chain(1)),
                 remote(PB.at[pl.ds(R0 + 1, 3), IN], HP_R.at[1], hs.at[7], hr.at[7], chain(-1))))

    def pre_pressure(i):
        div = diverge(1, i, sgn[i])
        DB[i] = div
        PB[i, IN] = PB[i, IN] - TAU * EB[i] * div

    rows(7, 17, pre_pressure)

    def residual(q, ii):
        v, total = stencil(U, 1, q, ii)
        w = PB[ii, IN]
        if q == 0:
            gp = PB[ii, UP] - PB[ii, DN]
        elif q == 1:
            gp = PB[ii + 1, IN] - PB[ii - 1, IN]
        else:
            gp = hi1(w) - lo1(w)
        res = -0.5 * gp - EB[ii] * (6.0 * v - total)
        return res + RAYLEIGH * TB[ii, IN] if q == 0 else res

    def send_vector(q):
        one = pl.ds(q, 1)
        out = [
            remote(CS.at[one], CR.at[1, one], xs.at[q, 1], xr.at[q, 1], chain(2)),
            remote(CS.at[one], CR.at[4, one], xs.at[q, 4], xr.at[q, 4], chain(-2)),
            remote(CS.at[one, pl.ds(1, 1)], CR.at[2, one, pl.ds(1, 1)], xs.at[q, 2], xr.at[q, 2], chain(3)),
            remote(CS.at[one, pl.ds(0, 1)], CR.at[5, one, pl.ds(0, 1)], xs.at[q, 5], xr.at[q, 5], chain(-3)),
            remote(CS.at[one], CR.at[0, one], xs.at[q, 0], xr.at[q, 0], chain(1)),
            remote(CS.at[one], CR.at[3, one], xs.at[q, 3], xr.at[q, 3], chain(-1)),
        ]
        for copy in out:
            copy.start()
        return out

    ex = []
    for q in range(3):
        vals = [cinv[m] * restrict(q, m, residual(q, R0 + 2 * m) + residual(q, R0 + 2 * m + 1)) for m in range(4)]
        pack(q, vals)
        ex.append(send_vector(q))
        for m in range(4):
            CU[0, q, C0 + m, CIN] = vals[m]
            CC[q, C0 + m] = vals[m]
    cg = [restrict(4, m, DB[R0 + 2 * m] + DB[R0 + 2 * m + 1]) for m in range(4)]
    pack(4, cg)
    ex.append(ex_e + send_scalar(4))
    for pair in (halo[3],) + tuple(halo[:3]):
        for copy in pair:
            copy.start()
    for m in range(4):
        CG[C0 + m] = cg[m]

    def unpack(x):
        return (jnp.where(even, x, pltpu.roll(x, 1, 1)), jnp.where(even, pltpu.roll(x, 127, 1), x))

    def take(n, f, h):
        turn = turned(cflip[n], cback)
        a, b = unpack(CR[n, f, h])
        return turn(a), turn(b)

    def csweep(s, q, i):
        v = CU[s, q, i, CIN]
        total = (CU[s, q, i, CUP] + CU[s, q, i, CDN]) + (CU[s, q, i + 1, CIN] + CU[s, q, i - 1, CIN])
        CU[1 - s, q, i, CIN] = A * v + B * (total + (lo2(v) + hi2(v))) + CC[q, i]

    def cdiverge(s, i):
        v = CU[s, 2, i, CIN]
        return 0.25 * ((CU[s, 0, i, CUP] - CU[s, 0, i, CDN]) + (CU[s, 1, i + 1, CIN] - CU[s, 1, i - 1, CIN])
                       + csgn[i] * (hi2(v) - lo2(v)))

    for q in range(3):
        for copy in ex[q]:
            copy.wait_recv()
        for n, base in ((0, -4), (3, 4), (1, -8), (4, 8)):
            for h in range(2):
                I = C0 + base + 2 * h
                for o, v in zip((I, I + 1), take(n, q, h)):
                    CU[0, q, o, CIN] = v
                    CC[q, o] = v
        CU[0, q, 0, CIN] = take(2, q, 1)[1]
        CU[0, q, 21, CIN] = take(5, q, 0)[0]
        rows(1, 21, lambda i: csweep(0, q, i))
        rows(2, 20, lambda i: csweep(1, q, i))

    for copy in ex[3]:
        copy.wait_recv()
    for n, I, h in ((0, -4, 0), (0, -2, 1), (3, 4, 0), (3, 6, 1), (1, -6, 1), (4, 8, 0)):
        for f, ref in ((3, CE), (4, CG)):
            ref[C0 + I], ref[C0 + I + 1] = take(n, f, h)

    def cpress1(i):
        CP[i, CIN] = -TAU * CE[i] * (cdiverge(0, i) + CG[i])

    rows(3, 19, cpress1)

    def cfirst(i):
        v = CP[i, CIN]
        scale = (-B) / CE[i]
        CC[0, i] = CC[0, i] + scale * (CP[i, CUP] - CP[i, CDN])
        CC[1, i] = CC[1, i] + scale * (CP[i + 1, CIN] - CP[i - 1, CIN])
        CC[2, i] = CC[2, i] + scale * (csgn[i] * (hi2(v) - lo2(v)))
        for q in range(3):
            csweep(0, q, i)

    rows(4, 18, cfirst)
    for q in range(3):
        rows(5, 17, lambda i: csweep(1, q, i))
    for q in range(3):
        rows(6, 16, lambda i: csweep(0, q, i))

    def spread(f, m, v):
        X[f, m, pl.ds(0, 8, stride=2)] = v
        X[f, m, pl.ds(1, 8, stride=2)] = v

    def back_up_p(i):
        spread(3, i - 7, CP[i, CIN] - TAU * CE[i] * (cdiverge(1, i) + CG[i]))

    rows(7, 15, back_up_p)
    turns = (turned(flip_l, back), turned(flip_r, back))
    for copy in halo[3]:
        copy.wait_recv()
    for side, prow in ((0, 4), (1, 17)):
        for n in range(3):
            PB[prow + n, IN] = turns[side](HP_R[side, n])

    def add_p(m):
        for n in range(2):
            PF[4 + 2 * m + n, IN] = PB[4 + 2 * m + n, IN] + X[3, m]

    rows(0, 8, add_p)

    mine = pl.ds(pl.multiple_of(r * 8, 8), 8)

    def place(f):
        return uo_ref.at[f] if f < 3 else po_ref

    def home(f, step):
        rt = jnp.where(r + step >= 4, r + step - 4, r + step)
        return remote(OUT.at[f, pl.ds(4 * rt, 4)], place(f).at[:, mine], os_.at[f, step], or_.at[f], (g, d, rt))

    def own(f):
        return pltpu.make_async_copy(OUT.at[f, layers], place(f).at[:, mine], ol.at[f])

    def send_home(f):
        for step in (2, 1, 3):
            home(f, step).start()
        own(f).start()

    for q in range(3):
        for copy in halo[q]:
            copy.wait_recv()
        for side, urow in ((0, 4), (1, 18)):
            for n in range(2):
                U[1, q, urow + n, IN] = turns[side](HU_R[side, q, n])
        rows(7, 15, lambda i: spread(q, i - 7, CU[1, q, i, CIN]))

        def add_u(m):
            for n in range(2):
                U[0, q, 4 + 2 * m + n, IN] = U[1, q, 4 + 2 * m + n, IN] + X[q, m]

        rows(0, 8, add_u)
        for copy in halo[q]:
            copy.wait_send()
        rows(5, 19, lambda i: push(PF, KB[i], q, i))
        rows(5, 19, lambda i: sweep(0, q, i))
        rows(6, 18, lambda i: sweep(1, q, i))
        rows(7, 17, lambda i: sweep(0, q, i))
        rows(0, 8, lambda a: set_column(OUT.at[q], a, U[1, q, R0 + a, IN]))
        send_home(q)

    def finish_p(a):
        i = R0 + a
        set_column(OUT.at[3], a, PF[i, IN] - TAU * EB[i] * diverge(1, i, 1.0))

    rows(0, 8, finish_p)
    send_home(3)

    def finish_t(a):
        i = R0 + a
        t = TB[i, IN]
        up, dn, nx, pv, hi, lo = TB[i, UP], TB[i, DN], TB[i + 1, IN], TB[i - 1, IN], hi1(t), lo1(t)
        lap = 6.0 * t - (((up + dn) + (nx + pv)) + (hi + lo))
        carried = 0.5 * (U[1, 0, i, IN] * (up - dn) + U[1, 1, i, IN] * (nx - pv) + U[1, 2, i, IN] * (hi - lo))
        set_column(to_ref, a, t + TIME_STEP * (-KAPPA * lap - carried))

    rows(0, 8, finish_t)

    for copy in halo[3]:
        copy.wait_send()
    for copy in heat:
        copy.wait_send()
    for n in range(5):
        for copy in lateral(n):
            copy.wait_send()
    for group in ex:
        for copy in group:
            copy.wait_send()
    for rt in range(4):
        @pl.when(r != rt)
        def _():
            for n in range(5):
                across(n, rt).wait_send()
    for f in range(4):
        for step in (2, 1, 3):
            home(f, step).wait_send()
        own(f).wait()
    for f in range(4):
        landed(place(f).at[:, pl.ds(0, 24)], or_.at[f])


def write_out(*refs):
    sem = refs[6]
    copies = [pltpu.make_async_copy(refs[n], refs[3 + n], sem.at[n]) for n in range(3)]
    for copy in copies:
        copy.start()
    for copy in copies:
        copy.wait()


def per_device(n_dia, n_chain, t, u, p, e, flags):
    f32 = jnp.float32
    V = pltpu.VMEM
    DMA = pltpu.SemaphoreType.DMA
    any_ = pl.BlockSpec(memory_space=pl.ANY)
    vmem = pl.BlockSpec(memory_space=pltpu.VMEM)
    done = pl.pallas_call(
        functools.partial(kernel, n_dia, n_chain, flags.shape[0]),
        out_shape=(
            V(u.shape, f32),
            V(p.shape, f32),
            V(t.shape, f32),
        ),
        in_specs=[any_] * 5,
        out_specs=(vmem,) * 3,
        scratch_shapes=[
            V((3, 16, 24, 128), f32), V((16, 24, 128), f32), V((16, 24, 128), f32), V((16, 24, 128), f32),
            V((2, 3, 24, 32, 128), f32), V((24, 32, 128), f32), V((24, 32, 128), f32),
            V((24, 16, 128), f32), V((24, 16, 128), f32), V((24, 32, 128), f32),
            V((3, 24, 16, 128), f32), V((24, 16, 128), f32), V((5, 4, 16, 128), f32),
            V((5, 2, 8, 128), f32), V((6, 5, 2, 8, 128), f32),
            V((2, 3, 22, 24, 128), f32), V((3, 22, 8, 128), f32), V((22, 8, 128), f32), V((22, 8, 128), f32),
            V((22, 24, 128), f32), V((4, 8, 16, 128), f32),
            V((2, 3, 2, 16, 128), f32), V((2, 3, 16, 128), f32),
            V((4, 16, 8, 128), f32),
            pltpu.SMEM(flags.shape, jnp.int32), pltpu.SMEM((24,), f32), pltpu.SMEM((22,), f32), pltpu.SMEM((6,), jnp.int32),
            DMA((6, 6)), DMA((11,)), DMA((6,)), DMA((8,)), DMA((8,)), DMA((5, 6)), DMA((5, 6)),
            DMA((4, 4)), DMA((4,)), DMA((4,)), DMA,
        ],
        compiler_params=pltpu.CompilerParams(collective_id=0, has_side_effects=True),
        name="cycle",
    )(t, u, p, e, flags)
    return pl.pallas_call(
        write_out,
        out_shape=[jax.ShapeDtypeStruct(x.shape, f32) for x in done],
        in_specs=[vmem] * 3,
        out_specs=[any_] * 3,
        scratch_shapes=[DMA((3,))],
        name="write_out",
    )(*[pltpu.with_memory_space_constraint(x, pltpu.VMEM) for x in done])


def solution(mesh):
    n_dia = mesh.shape["dia"]
    n_chain = n_dia * mesh.shape["grp"] * mesh.shape["rad"]
    return jax.shard_map(
        functools.partial(per_device, n_dia, n_chain),
        mesh=mesh,
        in_specs=(
            P(None, ("grp", "dia", "rad"), None),
            P(None, "rad", ("grp", "dia"), None),
            P("rad", ("grp", "dia"), None),
            P("rad", ("grp", "dia"), None),
            P(),
        ),
        out_specs=(
            P(None, "rad", ("grp", "dia"), None),
            P("rad", ("grp", "dia"), None),
            P(None, ("grp", "dia", "rad"), None),
        ),
        check_vma=False,
    )
```
